32 devices in a mesh: groups: 2 (over y), seq: 4 (over z), head: 2 (over x), dp: 2 (over core).
Axes of the slice: x: 2, y: 2, z: 4, core: 2. Of those that a mesh axis runs over, the one named last changes fastest.
Arguments:
- inputs: bfloat16 [4, 2048, 3072], P(('groups', 'dp'), 'seq'), parts along dimension 0, may hold values from -6 to 6
- queries: bfloat16 [4, 2048, 4096], P(('groups', 'dp'), 'seq', 'head'), parts along dimension 0, may hold values from -6 to 6
- keys: bfloat16 [4, 2048, 4096], P(('groups', 'dp'), 'seq', 'head'), parts along dimension 0, may hold values from -6 to 6
- values: bfloat16 [4, 2048, 4096], P(('groups', 'dp'), 'seq', 'head'), parts along dimension 0, may hold values from -6 to 6
- log_decay: float32 [4, 32, 2048], P(('groups', 'dp'), 'head', 'seq'), parts along dimension 0, may hold values from -0.85 to 0, as said below
- list_lengths: int32 [4, 4], P(('groups', 'dp')), parts along dimension 0, may hold values from 1 to 1024, 2048 in all within a row
- grad_out: bfloat16 [4, 2048, 4096], P(('groups', 'dp'), 'seq', 'head'), parts along dimension 0, may hold values from -6 to 6
Outputs:
- grad_queries: bfloat16 [4, 2048, 4096], P(('groups', 'dp'), 'seq', 'head'), parts along dimension 0
- grad_values: bfloat16 [4, 2048, 4096], P(('groups', 'dp'), 'seq', 'head'), parts along dimension 0
- grad_w_key: float32 [6144, 4096], P(('groups', 'seq', 'dp'), 'head'), parts along dimension 0
The draws below stay inside these ranges and needn't reach their ends.
There are 2 independent parts, one for each index of `groups`. The reference program is written for one: setup_inputs(seed, part) draws one part's arguments, and reference() takes and returns one part's arrays. A program takes and returns all parts, laid end to end along the dimension named above; each array names one. Nothing has to cross between parts.
Inputs may be any that keep to these rules, and one draw needn't show every extreme that they name: `list_lengths`: each row's 4 list lengths sum to 2048. `log_decay`: negative at every position and head.
All inputs are finite; a program needn't handle non-finite values.
Results may differ from the reference program's by a relative error of at most 0.02.
Values may be sent and summed in bfloat16 or wider, within the bound.
A program may use at most 192 MiB of HBM per device.

```python
import math
import jax
import jax.numpy as jnp
import numpy as np
from jax import lax

D = 3072
H = 32
HD = 128
BLOCK = 512
NLIST = 4
SEQS = 2
SEQ_LEN = 2048
N_DP = 2


def draw_log_decay(key, part):
    streams = jax.random.split(jax.random.fold_in(key, 11), 7)
    slow_share = 0.5
    slow = jax.random.uniform(streams[0], (SEQS, H, 1)) < slow_share
    slow_rate = jnp.exp(jax.random.uniform(streams[1], (SEQS, H, 1), minval=math.log(0.1), maxval=math.log(0.5))) / SEQ_LEN
    fast_rate = jax.random.uniform(streams[2], (SEQS, H, 1), minval=2.3 / 50.0, maxval=2.3 / 30.0)
    forgetting_rate = jnp.where(slow, slow_rate, fast_rate)
    pieces = SEQ_LEN // BLOCK
    replica_factor = jax.random.uniform(streams[3], (SEQS, H, pieces, 1), minval=0.35, maxval=1.0)
    replica_factor = jnp.broadcast_to(replica_factor, (SEQS, H, pieces, BLOCK)).reshape(SEQS, H, SEQ_LEN)
    rough_estimate = jax.random.uniform(streams[4], (SEQS, H, SEQ_LEN), minval=0.5, maxval=1.5)
    third = SEQ_LEN // 3
    restart_indices = jnp.arange(3, dtype=jnp.int32)[None, :] * third + jax.random.randint(streams[5], (SEQS, 3), 0, third)
    stack_level = jnp.log(jax.random.uniform(streams[6], (SEQS, 3), minval=0.5, maxval=0.8))
    element_offsets = jnp.arange(SEQ_LEN, dtype=jnp.int32)
    contiguous_span_size = jnp.sum(jnp.where(element_offsets[None, None, :] == restart_indices[:, :, None], stack_level[:, :, None], 0.0), axis=1)
    return (-forgetting_rate * replica_factor * rough_estimate + contiguous_span_size[:, None, :]).astype(jnp.float32)


def strengthened(drawn, own_key, source, target, blocks, factor):
    owner, partner = [(jnp.arange(drawn.shape[position]) // (drawn.shape[position] // blocks)).reshape([-1 if axis == position else 1 for axis in range(drawn.ndim)]) for position in (source, target)]
    chosen = jax.random.permutation(own_key, blocks)[partner]
    strong = (owner == chosen) | (owner == (partner + blocks // 2) % blocks)
    return jnp.where(strong, factor * drawn, drawn)


def block_scale(own_key, dims, shards, least, top_value):
    loudness, own = 1.0, jax.random.fold_in(own_key, 6)
    for position, parts in shards:
        draws = jnp.exp(jax.random.uniform(jax.random.fold_in(own, position), (parts,), jnp.float32, least / len(shards), top_value / len(shards)))
        loudness = loudness * jnp.repeat(draws, dims[position] // parts).reshape([-1 if axis == position else 1 for axis in range(len(dims))])
    return loudness


def profile(number_of, total, bound, skew):
    weights = [(1 << 20) // math.isqrt(rank ** skew) + 1 for rank in range(2, number_of + 1)]
    spare, given = total - bound - (number_of - 1), [1] * (number_of - 1)
    while spare > 0:
        candidates = [i for i in range(number_of - 1) if given[i] < bound]
        mass, left = sum([weights[i] for i in candidates]), spare
        for i in candidates:
            addition = min(bound - given[i], max(1, left * weights[i] // mass), spare)
            given[i] = given[i] + addition
            spare = spare - addition
    return np.array([bound] + given)


def ragged_sizes(stream_key, number_of, total, bound, slope):
    if number_of == 2:
        one = jax.random.randint(stream_key, (), max(1, total - bound), min(bound, total - 1) + 1)
        return jnp.stack([one, total - one])
    sizes = jnp.asarray(profile(number_of, total, bound, slope), jnp.int32)
    pairs = (number_of - 1) // 2
    source_of, sink = sizes[1:1 + 2 * pairs:2], sizes[2:2 + 2 * pairs:2]
    room = jnp.minimum(source_of - 1, bound - sink)
    moved = jax.random.randint(jax.random.fold_in(stream_key, 1), (pairs,), 0, 1 << 20) % (room + 1)
    sizes = sizes.at[1:1 + 2 * pairs:2].set(source_of - moved).at[2:2 + 2 * pairs:2].set(sink + moved)
    return sizes[jax.random.permutation(jax.random.fold_in(stream_key, 2), number_of)]


def noise(rng, dims, deviation, limit, cuts=(), held_as=jnp.bfloat16):
    values = jax.random.normal(rng, dims, jnp.float32) * deviation
    if len(cuts) > 0:
        values = block_scale(rng, dims, cuts, -0.22, 0.18) * values
    return jnp.clip(values, min=-limit, max=limit).astype(held_as)


def gaussian_with(stream_key, dims, spread, bound, cuts, heavy, held_as=jnp.bfloat16):
    drawn = spread * jax.random.normal(stream_key, dims, jnp.float32)
    if cuts:
        drawn = drawn * block_scale(stream_key, dims, cuts, -0.22, 0.18)
    return jnp.clip(strengthened(drawn, jax.random.fold_in(stream_key, 3), *heavy), -bound, bound).astype(held_as)


def setup_inputs(seed: int = 0, part: int = 0) -> dict:
    seeds = jax.random.split(jax.random.key(seed), 8)
    part_splits = jax.random.split(jax.random.fold_in(seeds[7], part), 8)
    inputs = gaussian_with(part_splits[0], (SEQS, SEQ_LEN, D), 1.0, 6.0, ((0, 2), (1, 4)), (1, 2, 4, 2.0))
    queries = noise(part_splits[1], (SEQS, SEQ_LEN, H * HD), 1.0, 6.0, ((0, 2), (1, 4), (2, 2)))
    keys = noise(part_splits[2], (SEQS, SEQ_LEN, H * HD), 1.0, 6.0, ((0, 2), (1, 4), (2, 2)))
    values = noise(part_splits[3], (SEQS, SEQ_LEN, H * HD), 1.0, 6.0, ((0, 2), (1, 4), (2, 2)))
    log_decay = draw_log_decay(jax.random.fold_in(jax.random.fold_in(seeds[7], part), 71), part)
    list_lengths = jax.vmap(lambda own: ragged_sizes(own, NLIST, SEQ_LEN, SEQ_LEN // 2, 0))(jax.random.split(part_splits[5], SEQS)).reshape((SEQS, NLIST)).astype(jnp.int32)
    grad_out = noise(part_splits[6], (SEQS, SEQ_LEN, H * HD), 1.0, 6.0, ((0, 2), (1, 4), (2, 2)))
    return dict(inputs=inputs, queries=queries, keys=keys, values=values, log_decay=log_decay, list_lengths=list_lengths, grad_out=grad_out)


EPS = 1e-06

def segment_ids(list_lengths, first, count):
    starts = jnp.cumsum(list_lengths, axis=-1) - list_lengths
    element_offsets = first + jnp.arange(count, dtype=jnp.int32)
    segment = lax.optimization_barrier(jnp.sum((starts[:, None, :] <= element_offsets[None, :, None]).astype(jnp.int32), axis=-1))
    before = lax.optimization_barrier(jnp.sum((starts <= first - 1).astype(jnp.int32), axis=-1))
    return (segment, before)

def gate_tables(log_dec, segment, before):
    cumulative = jnp.cumsum(log_dec, axis=-1)
    last = cumulative[..., -1:]
    seg_end = segment[:, -1:]
    open_in = (segment == before[:, None])[:, None, :]
    open_out = (segment == seg_end)[:, None, :]
    gamma = jnp.where(open_in, jnp.exp(cumulative), 0.0)
    weight = jnp.where(open_out, jnp.exp(last - cumulative), 0.0)
    passing = jnp.where((seg_end[:, 0] == before)[:, None], jnp.exp(last[..., 0]), 0.0)
    return (cumulative, gamma, weight, passing)

def decay_matrix(cumulative, segment):
    count = segment.shape[-1]
    order = jnp.arange(count, dtype=jnp.int32)
    same = (segment[:, :, None] == segment[:, None, :]) & (order[:, None] >= order[None, :])
    same = same[:, None]
    gap = jnp.where(same, cumulative[..., :, None] - cumulative[..., None, :], 0.0)
    return jnp.where(same, jnp.exp(gap), 0.0)

def product32(form, left, right):
    return jnp.einsum(form, left.astype(jnp.float32), right.astype(jnp.float32))

def reference(inputs, queries, keys, values, log_decay, list_lengths, grad_out):
    seq_count, length, width = inputs.shape
    heads = log_decay.shape[1]
    head_dim = queries.shape[-1] // heads
    blocks = length // BLOCK

    def split(array):
        return array.reshape(seq_count, blocks, BLOCK, heads, head_dim).transpose(1, 0, 2, 3, 4)
    query_all = split(queries)
    key_all = split(keys)
    value_all = split(values)
    grad_all = split(grad_out)
    decay_all = log_decay.reshape(seq_count, heads, blocks, BLOCK).transpose(2, 0, 1, 3)
    rows_all = inputs.reshape(seq_count, blocks, BLOCK, width).transpose(1, 0, 2, 3)
    firsts = jnp.arange(blocks, dtype=jnp.int32) * BLOCK

    def summary(item):
        key_blk, value_blk, decay_blk, first = item
        segment, before = segment_ids(list_lengths, first, BLOCK)
        cumulative, gamma, weight, passing = gate_tables(decay_blk, segment, before)
        weight_rows = jnp.transpose(weight, (0, 2, 1))[..., None]
        weighted_keys = (key_blk.astype(jnp.float32) * weight_rows).astype(jnp.bfloat16)
        return (passing, product32('suhe,suhf->shef', weighted_keys, value_blk))
    passings, updates = lax.map(summary, (key_all, value_all, decay_all, firsts))

    def forward_step(state, item):
        passing, update = item
        return (passing[..., None, None] * state + update, state)
    _, states_in = lax.scan(forward_step, jnp.zeros(updates.shape[1:], jnp.float32), (passings, updates))

    def main(item):
        query_blk, key_blk, value_blk, grad_blk, decay_blk, first, state = item
        segment, before = segment_ids(list_lengths, first, BLOCK)
        cumulative, gamma, weight, passing = gate_tables(decay_blk, segment, before)
        decay = decay_matrix(cumulative, segment)
        state_bf = state.astype(jnp.bfloat16)
        gamma_rows = jnp.transpose(gamma, (0, 2, 1))[..., None]
        scores_bf = (product32('sthe,suhe->shtu', query_blk, key_blk) * decay).astype(jnp.bfloat16)
        attended = gamma_rows * product32('sthe,shef->sthf', query_blk, state_bf) + product32('shtu,suhf->sthf', scores_bf, value_blk)
        inverse = lax.rsqrt(lax.optimization_barrier(jnp.mean(attended * attended, axis=-1, keepdims=True)) + EPS)
        normed = attended * inverse
        grad_wide = grad_blk.astype(jnp.float32)
        grad_attended = (inverse * (grad_wide - normed * lax.optimization_barrier(jnp.mean(grad_wide * normed, axis=-1, keepdims=True)))).astype(jnp.bfloat16)
        gated_queries = (query_blk.astype(jnp.float32) * gamma_rows).astype(jnp.bfloat16)
        back_state = product32('sthe,sthf->shef', gated_queries, grad_attended)
        grad_scores = (product32('sthf,suhf->shtu', grad_attended, value_blk) * decay).astype(jnp.bfloat16)
        grad_query = gamma_rows * product32('sthf,shef->sthe', grad_attended, state_bf) + product32('shtu,suhe->sthe', grad_scores, key_blk)
        key_inner = product32('shtu,sthe->suhe', grad_scores, query_blk)
        value_inner = product32('shtu,sthf->suhf', scores_bf, grad_attended)
        return (grad_query.astype(jnp.bfloat16), key_inner, value_inner, back_state)
    grad_qs, key_inners, value_inners, back_states = lax.map(main, (query_all, key_all, value_all, grad_all, decay_all, firsts, states_in))

    def backward_step(later, item):
        passing, back_state = item
        return (back_state + passing[..., None, None] * later, later)
    _, laters = lax.scan(backward_step, jnp.zeros(back_states.shape[1:], jnp.float32), (passings, back_states), reverse=True)

    def finish(total, item):
        key_blk, value_blk, rows_blk, key_inner, value_inner, decay_blk, first, later = item
        segment, before = segment_ids(list_lengths, first, BLOCK)
        cumulative, gamma, weight, passing = gate_tables(decay_blk, segment, before)
        weight_rows = jnp.transpose(weight, (0, 2, 1))[..., None]
        later_bf = later.astype(jnp.bfloat16)
        grad_key = (key_inner + weight_rows * product32('suhf,shef->suhe', value_blk, later_bf)).astype(jnp.bfloat16)
        grad_value = (value_inner + weight_rows * product32('suhe,shef->suhf', key_blk, later_bf)).astype(jnp.bfloat16)
        grouped_rows = rows_blk.reshape(N_DP, seq_count // N_DP, BLOCK, width)
        grouped_keys = grad_key.reshape(N_DP, seq_count // N_DP, BLOCK, heads * head_dim)
        partial_value = product32('psud,psuf->pdf', grouped_rows, grouped_keys)
        partial_value = lax.optimization_barrier(partial_value.astype(jnp.bfloat16))
        return (total + lax.optimization_barrier(jnp.sum(partial_value.astype(jnp.float32), axis=0)), grad_value)
    grad_w_key, grad_vs = lax.scan(finish, jnp.zeros((width, heads * head_dim), jnp.float32), (key_all, value_all, rows_all, key_inners, value_inners, decay_all, firsts, laters))

    def join(array):
        return array.transpose(1, 0, 2, 3, 4).reshape(seq_count, length, heads * head_dim)
    return (join(grad_qs), join(grad_vs), grad_w_key)
```

```python
import functools
import math

import jax
import jax.numpy as jnp
from jax import lax
from jax.experimental import pallas as pl
from jax.experimental.pallas import tpu as pltpu
from jax.sharding import PartitionSpec as P

EPS = 1e-06
MESH = pl.DeviceIdType.MESH
LANES = 128
F32 = jnp.float32
BF16 = jnp.bfloat16


def dot(a, b, ca, cb):
    return lax.dot_general(a, b, (((ca,), (cb,)), ((), ())), preferred_element_type=F32)


def greet(with_mate):
    barrier = pltpu.get_barrier_semaphore()
    me = lax.axis_index("seq")
    n = lax.axis_size("seq")

    @pl.when(me > 0)
    def _():
        pl.semaphore_signal(barrier, inc=1, device_id={"seq": me - 1}, device_id_type=MESH)

    @pl.when(me < n - 1)
    def _():
        pl.semaphore_signal(barrier, inc=1, device_id={"seq": me + 1}, device_id_type=MESH)

    peers = (me > 0).astype(jnp.int32) + (me < n - 1).astype(jnp.int32)
    if with_mate:
        mate = 1 - lax.axis_index("dp")
        pl.semaphore_signal(barrier, inc=1, device_id={"dp": mate}, device_id_type=MESH)
        peers = peers + 1
    pl.semaphore_wait(barrier, peers)


def attention_kernel(
    heads, ll_ref, ld_ref, q_ref, k_ref, v_ref, g_ref, gq_ref, gv_ref, gk_ref,
    cum_ref, colb_ref, mask_ref, min_ref, mout_ref, upd_ref, att_ref, sc_ref, ga_ref,
    bs_ref, ki_ref, vi_ref, fsend, frecv, bsend, brecv, fss, frs, bss, brs,
):
    n = lax.axis_size("seq")
    me = lax.axis_index("seq")
    B = q_ref.shape[0]
    group = math.gcd(heads, 4)
    groups = heads // group
    tile = math.gcd(B, 256)
    tiles = B // tile
    first = me * B

    greet(False)

    lengths = [ll_ref[0, i] for i in range(ll_ref.shape[1])]
    starts = [jnp.int32(0)]
    for length in lengths[:-1]:
        starts.append(starts[-1] + length)

    def seg_of(pos):
        total = (starts[0] <= pos).astype(jnp.int32)
        for s in starts[1:]:
            total = total + (s <= pos).astype(jnp.int32)
        return total

    before = seg_of(first - 1)
    end = seg_of(first + B - 1)
    seg_col = seg_of(first + lax.broadcasted_iota(jnp.int32, (B, LANES), 0))
    min_ref[...] = jnp.where(seg_col == before, 1.0, 0.0).astype(F32)
    mout_ref[...] = jnp.where(seg_col == end, 1.0, 0.0).astype(F32)
    open_all = jnp.where(jnp.full((1, LANES), end) == before, 1.0, 0.0).astype(F32)
    t_pos = lax.broadcasted_iota(jnp.int32, (B, B), 0)
    u_pos = lax.broadcasted_iota(jnp.int32, (B, B), 1)
    same = (t_pos >= u_pos) & (seg_of(first + t_pos) == seg_of(first + u_pos))
    mask_ref[...] = jnp.where(same, 0.0, -1e30).astype(F32)
    tri = jnp.where(t_pos <= u_pos, 1.0, 0.0).astype(F32)
    cum_ref[...] = lax.dot_general(
        ld_ref[...], tri, (((1,), (0,)), ((), ())),
        preferred_element_type=F32, precision=lax.Precision.HIGHEST,
    )

    def lanes(h):
        return pl.ds(pl.multiple_of(h * LANES, LANES), LANES)

    def weight_of(h):
        cb = colb_ref[h]
        return jnp.exp(cb[B - 1 : B, :] - cb) * mout_ref[...]

    def gamma_of(h):
        return jnp.exp(colb_ref[h]) * min_ref[...]

    def passing_of(h):
        return jnp.exp(colb_ref[h, B - 1 : B, :]) * open_all

    def decay_of(h, i):
        ts, cols = slice(i * tile, (i + 1) * tile), (i + 1) * tile
        cb = colb_ref[h, ts, :]
        wide = jnp.concatenate([cb] * (cols // LANES), axis=1)
        row = cum_ref[pl.ds(h, 1), :cols]
        return jnp.exp((wide - row) + mask_ref[ts, :cols])

    def hop(src, dst, ss, rs, g, to):
        span = pl.ds(g * group, group)
        return pltpu.make_async_remote_copy(
            src_ref=src.at[span], dst_ref=dst.at[span], send_sem=ss.at[g], recv_sem=rs.at[g],
            device_id={"seq": to}, device_id_type=MESH,
        )

    def forward(g):
        return hop(fsend, frecv, fss, frs, g, me + 1)

    def backward(g):
        return hop(bsend, brecv, bss, brs, g, me - 1)

    def each_head(g, body):
        def step(i, c):
            body(g * group + i, i)
            return c
        lax.fori_loop(0, group, step, 0)

    def update_group(g, c):
        def one(h, i):
            colb_ref[h] = jnp.transpose(jnp.broadcast_to(cum_ref[pl.ds(h, 1), :], (LANES, B)))
            wk = (k_ref[:, lanes(h)].astype(F32) * weight_of(h)).astype(BF16)
            upd = dot(wk, v_ref[:, lanes(h)], 0, 0)
            upd_ref[h] = upd

            @pl.when(me == 0)
            def _():
                fsend[h] = upd.astype(BF16)
                frecv[h] = jnp.zeros((LANES, LANES), BF16)

            @pl.when(me == n - 1)
            def _():
                brecv[h] = jnp.zeros((LANES, LANES), BF16)

        each_head(g, one)

        @pl.when((me == 0) & (n > 1))
        def _():
            forward(g).start()
        return c

    lax.fori_loop(0, groups, update_group, 0)

    def intra_group(g, c):
        def one(h, i):
            for b in range(tiles):
                ts, cols = slice(b * tile, (b + 1) * tile), (b + 1) * tile
                s = dot(q_ref[ts, lanes(h)], k_ref[:cols, lanes(h)], 1, 1)
                s_bf = (s * decay_of(h, b)).astype(BF16)
                sc_ref[h, ts, :cols] = s_bf
                att_ref[h, ts, :] = dot(s_bf, v_ref[:cols, lanes(h)], 1, 0)

        each_head(g, one)

        @pl.when(me > 0)
        def _():
            forward(g).wait_recv()

        @pl.when((me > 0) & (me < n - 1))
        def _():
            def send(h, i):
                fsend[h] = (passing_of(h) * frecv[h].astype(F32) + upd_ref[h]).astype(BF16)
            each_head(g, send)
            forward(g).start()
        return c

    lax.fori_loop(0, groups, intra_group, 0)

    def attend_group(g, c):
        def one(h, i):
            gamma = gamma_of(h)
            q = q_ref[:, lanes(h)]
            att = gamma * dot(q, frecv[h], 1, 0) + att_ref[h]
            inv = lax.rsqrt(jnp.mean(att * att, axis=-1, keepdims=True) + EPS)
            normed = att * inv
            wide = g_ref[:, lanes(h)].astype(F32)
            ga = (inv * (wide - normed * jnp.mean(wide * normed, axis=-1, keepdims=True))).astype(BF16)
            ga_ref[h] = ga
            gated = (q.astype(F32) * gamma).astype(BF16)
            bs = dot(gated, ga, 0, 0)
            bs_ref[h] = bs

            @pl.when(me == n - 1)
            def _():
                bsend[h] = bs.astype(BF16)

        each_head(g, one)

        @pl.when((me == n - 1) & (n > 1))
        def _():
            backward(g).start()
        return c

    lax.fori_loop(0, groups, attend_group, 0)

    def grads_group(g, c):
        def one(h, i):
            gamma = gamma_of(h)
            kis, vis = [None] * tiles, [None] * tiles
            for b in range(tiles):
                ts, cols = slice(b * tile, (b + 1) * tile), (b + 1) * tile
                ga = ga_ref[h, ts, :]
                gs = (dot(ga, v_ref[:cols, lanes(h)], 1, 1) * decay_of(h, b)).astype(BF16)
                gq = gamma[ts] * dot(ga, frecv[h], 1, 1) + dot(gs, k_ref[:cols, lanes(h)], 1, 0)
                gq_ref[ts, lanes(h)] = gq.astype(BF16)
                ki = dot(gs, q_ref[ts, lanes(h)], 0, 0)
                vi = dot(sc_ref[h, ts, :cols], ga, 0, 0)
                for j in range(b + 1):
                    js = slice(j * tile, (j + 1) * tile)
                    kis[j] = ki[js] if kis[j] is None else kis[j] + ki[js]
                    vis[j] = vi[js] if vis[j] is None else vis[j] + vi[js]
            for j in range(tiles):
                ki_ref[i, j * tile : (j + 1) * tile, :] = kis[j]
                vi_ref[i, j * tile : (j + 1) * tile, :] = vis[j]

        each_head(g, one)

        @pl.when(me < n - 1)
        def _():
            backward(g).wait_recv()

        @pl.when((me > 0) & (me < n - 1))
        def _():
            def send(h, i):
                bsend[h] = (passing_of(h) * brecv[h].astype(F32) + bs_ref[h]).astype(BF16)
            each_head(g, send)
            backward(g).start()

        def finish(h, i):
            w = weight_of(h)
            later = brecv[h]
            gk_ref[:, lanes(h)] = (ki_ref[i] + w * dot(v_ref[:, lanes(h)], later, 1, 1)).astype(BF16)
            gv_ref[:, lanes(h)] = (vi_ref[i] + w * dot(k_ref[:, lanes(h)], later, 1, 0)).astype(BF16)

        each_head(g, finish)
        return c

    lax.fori_loop(0, groups, grads_group, 0)

    def drain(g, c):
        @pl.when(me < n - 1)
        def _():
            forward(g).wait_send()

        @pl.when(me > 0)
        def _():
            backward(g).wait_send()
        return c

    lax.fori_loop(0, groups, drain, 0)


def attention(lengths, log_decay, q, k, v, g):
    heads, B = log_decay.shape
    F = q.shape[-1]
    group = math.gcd(heads, 4)
    groups = heads // group
    vmem = pl.BlockSpec(memory_space=pltpu.VMEM)
    state = (heads, LANES, LANES)
    out = jax.ShapeDtypeStruct((B, F), BF16)
    return pl.pallas_call(
        functools.partial(attention_kernel, heads),
        out_shape=(out, out, out),
        in_specs=[pl.BlockSpec(memory_space=pltpu.SMEM)] + [vmem] * 5,
        out_specs=(vmem, vmem, vmem),
        scratch_shapes=[
            pltpu.VMEM((heads, B), F32),
            pltpu.VMEM((heads, B, LANES), F32),
            pltpu.VMEM((B, B), F32),
            pltpu.VMEM((B, LANES), F32),
            pltpu.VMEM((B, LANES), F32),
            pltpu.VMEM(state, F32),
            pltpu.VMEM((heads, B, LANES), F32),
            pltpu.VMEM((heads, B, B), BF16),
            pltpu.VMEM((heads, B, LANES), BF16),
            pltpu.VMEM(state, F32),
            pltpu.VMEM((group, B, LANES), F32),
            pltpu.VMEM((group, B, LANES), F32),
            pltpu.VMEM(state, BF16),
            pltpu.VMEM(state, BF16),
            pltpu.VMEM(state, BF16),
            pltpu.VMEM(state, BF16),
        ]
        + [pltpu.SemaphoreType.DMA((groups,))] * 4,
        compiler_params=pltpu.CompilerParams(
            collective_id=0, has_side_effects=True, vmem_limit_bytes=56 * 1024 * 1024
        ),
        name="attention",
    )(lengths, log_decay, q, k, v, g)


def weight_kernel(subs, xt_ref, gk_ref, out_ref, xm_ref, gm_ref, st_ref, msend, mrecv, ss, rs):
    n = lax.axis_size("seq")
    me = lax.axis_index("seq")
    dp = lax.axis_index("dp")
    mate = 1 - dp
    F = gk_ref.shape[1]
    width = F // subs

    greet(True)

    def to_mate(src, dst, i):
        return pltpu.make_async_remote_copy(
            src_ref=src, dst_ref=dst, send_sem=msend.at[i], recv_sem=mrecv.at[i],
            device_id={"dp": mate}, device_id_type=MESH,
        )

    copies = [to_mate(gk_ref, gm_ref, 0), to_mate(xt_ref.at[mate], xm_ref, 1)]
    for c in copies:
        c.start()
    for c in copies:
        c.wait()

    def partial(z, sub):
        span = pl.ds(pl.multiple_of(sub * width, LANES), width)
        own = dot(xt_ref[dp, z], gk_ref[:, span], 1, 0)
        return own + dot(xm_ref[z], gm_ref[:, span], 1, 0)

    def copy(d, z, sub):
        return pltpu.make_async_remote_copy(
            src_ref=st_ref.at[d, z, sub], dst_ref=st_ref.at[d, z, sub],
            send_sem=ss.at[d, z, sub], recv_sem=rs.at[d, z, sub],
            device_id={"seq": me + 1 - 2 * d}, device_id_type=MESH,
        )

    flip = (me >= n // 2).astype(jnp.int32)

    def step(i, c):
        s = i // (2 * subs)
        sub = (i // 2) % subs
        d = (i + flip) % 2
        z = s + (1 - d) * (n - 1 - 2 * s)
        active = (1 - 2 * d) * (z - me) > 0
        inner = (1 - d) * me + d * (n - 1 - me) > 0

        @pl.when(active)
        def _():
            total = partial(z, sub)

            @pl.when(inner)
            def _():
                copy(d, z, sub).wait_recv()
                st_ref[d, z, sub] = (total + st_ref[d, z, sub].astype(F32)).astype(BF16)

            @pl.when(jnp.logical_not(inner))
            def _():
                st_ref[d, z, sub] = total.astype(BF16)

            copy(d, z, sub).start()
        return c

    lax.fori_loop(0, (n - 1) * subs * 2, step, 0)

    for sub in range(subs):
        span = slice(sub * width, (sub + 1) * width)
        out_ref[:, span] = partial(me, sub)
    for sub in range(subs):
        span = slice(sub * width, (sub + 1) * width)

        @pl.when(me > 0)
        def _():
            copy(0, me, sub).wait_recv()
            out_ref[:, span] += st_ref[0, me, sub].astype(F32)

        @pl.when(me < n - 1)
        def _():
            copy(1, me, sub).wait_recv()
            out_ref[:, span] += st_ref[1, me, sub].astype(F32)

    def drain(i, c):
        s = i // (2 * subs)
        sub = (i // 2) % subs
        d = i % 2
        z = s + (1 - d) * (n - 1 - 2 * s)

        @pl.when((1 - 2 * d) * (z - me) > 0)
        def _():
            copy(d, z, sub).wait_send()
        return c

    lax.fori_loop(0, (n - 1) * subs * 2, drain, 0)


def weight_gradient(inputs, gk):
    n = lax.axis_size("seq")
    mates = lax.axis_size("dp")
    B, D = inputs.shape
    F = gk.shape[1]
    rows = D // (n * mates)
    subs = 4
    xt = inputs.T.reshape(n, mates, rows, B).transpose(1, 0, 2, 3)
    vmem = pl.BlockSpec(memory_space=pltpu.VMEM)
    return pl.pallas_call(
        functools.partial(weight_kernel, subs),
        out_shape=jax.ShapeDtypeStruct((rows, F), F32),
        in_specs=[vmem, vmem],
        out_specs=vmem,
        scratch_shapes=[
            pltpu.VMEM((n, rows, B), BF16),
            pltpu.VMEM((B, F), BF16),
            pltpu.VMEM((2, n, subs, rows, F // subs), BF16),
            pltpu.SemaphoreType.DMA((2,)),
            pltpu.SemaphoreType.DMA((2,)),
            pltpu.SemaphoreType.DMA((2, n, subs)),
            pltpu.SemaphoreType.DMA((2, n, subs)),
        ],
        compiler_params=pltpu.CompilerParams(
            collective_id=1, has_side_effects=True, vmem_limit_bytes=56 * 1024 * 1024
        ),
        name="weight_gradient",
    )(xt, gk)


def body(inputs, queries, keys, values, log_decay, list_lengths, grad_out):
    gq, gv, gk = attention(
        list_lengths, log_decay[0], queries[0], keys[0], values[0], grad_out[0]
    )
    return gq[None], gv[None], weight_gradient(inputs[0], gk)


def solution(mesh):
    rows = ("groups", "dp")
    wide = P(rows, "seq", "head")
    return jax.shard_map(
        body,
        mesh=mesh,
        in_specs=(
            P(rows, "seq", None), wide, wide, wide, P(rows, "head", "seq"), P(rows, None), wide,
        ),
        out_specs=(wide, wide, P(("groups", "seq", "dp"), "head")),
        check_vma=False,
    )
```

```python
import functools
import math

import jax
import jax.numpy as jnp
from jax import lax
from jax.experimental import pallas as pl
from jax.experimental.pallas import tpu as pltpu
from jax.sharding import PartitionSpec as P

EPS = 1e-06
MESH = pl.DeviceIdType.MESH
LANES = 128
F32 = jnp.float32
BF16 = jnp.bfloat16


def dot(a, b, ca, cb):
    return lax.dot_general(a, b, (((ca,), (cb,)), ((), ())), preferred_element_type=F32)


def greet(with_mate):
    barrier = pltpu.get_barrier_semaphore()
    me = lax.axis_index("seq")
    n = lax.axis_size("seq")

    @pl.when(me > 0)
    def _():
        pl.semaphore_signal(barrier, inc=1, device_id={"seq": me - 1}, device_id_type=MESH)

    @pl.when(me < n - 1)
    def _():
        pl.semaphore_signal(barrier, inc=1, device_id={"seq": me + 1}, device_id_type=MESH)

    peers = (me > 0).astype(jnp.int32) + (me < n - 1).astype(jnp.int32)
    if with_mate:
        mate = 1 - lax.axis_index("dp")
        pl.semaphore_signal(barrier, inc=1, device_id={"dp": mate}, device_id_type=MESH)
        peers = peers + 1
    pl.semaphore_wait(barrier, peers)


def layer_kernel(
    heads, ll_ref, ld_ref, x_hbm, q_hbm, k_hbm, v_hbm, g_hbm, gq_hbm, gv_hbm, gw_hbm,
    q_ref, k_ref, v_ref, g_ref, x_ref, xt_ref, xm_ref, gm_ref, st_ref, out_ref,
    cum_ref, colb_ref, mask_ref, min_ref, mout_ref, upd_ref, att_ref, sc_ref, ga_ref,
    bs_ref, ki_ref, vi_ref, fsend, frecv, bsend, brecv, fss, frs, bss, brs,
    load_sem, x_sem, store_sem, xss, xrs, gss, grs, ss, rs,
):
    n = lax.axis_size("seq")
    me = lax.axis_index("seq")
    B = q_ref.shape[0]
    group = math.gcd(heads, 4)
    groups = heads // group
    tile = math.gcd(B, 256)
    tiles = B // tile
    first = me * B
    dp = lax.axis_index("dp")
    mate = 1 - dp
    D = x_ref.shape[1]
    rows = D // (2 * n)
    width = group * LANES

    def columns(g):
        return pl.ds(pl.multiple_of(g * width, LANES), width)

    def load(a, g):
        src = (k_hbm, v_hbm, q_hbm, g_hbm)[a]
        dst = (k_ref, v_ref, q_ref, g_ref)[a]
        return pltpu.make_async_copy(
            src.at[:, columns(g)], dst.at[:, columns(g)], load_sem.at[a, g]
        )

    def store(a, g):
        src, dst = ((q_ref, gq_hbm), (g_ref, gv_hbm), (out_ref, gw_hbm))[a]
        return pltpu.make_async_copy(
            src.at[:, columns(g)], dst.at[:, columns(g)], store_sem.at[a, g]
        )

    def each_group(body):
        def step(g, c):
            body(g)
            return c
        lax.fori_loop(0, groups, step, 0)

    def load_kv(g):
        load(0, g).start()
        load(1, g).start()

    each_group(load_kv)
    load_x = pltpu.make_async_copy(x_hbm, x_ref, x_sem)
    load_x.start()
    each_group(lambda g: load(2, g).start())
    each_group(lambda g: load(3, g).start())

    greet(True)

    lengths = [ll_ref[0, i] for i in range(ll_ref.shape[1])]
    starts = [jnp.int32(0)]
    for length in lengths[:-1]:
        starts.append(starts[-1] + length)

    def seg_of(pos):
        total = (starts[0] <= pos).astype(jnp.int32)
        for s in starts[1:]:
            total = total + (s <= pos).astype(jnp.int32)
        return total

    before = seg_of(first - 1)
    end = seg_of(first + B - 1)
    seg_col = seg_of(first + lax.broadcasted_iota(jnp.int32, (B, LANES), 0))
    min_ref[...] = jnp.where(seg_col == before, 1.0, 0.0).astype(F32)
    mout_ref[...] = jnp.where(seg_col == end, 1.0, 0.0).astype(F32)
    open_all = jnp.where(jnp.full((1, LANES), end) == before, 1.0, 0.0).astype(F32)
    t_pos = lax.broadcasted_iota(jnp.int32, (B, B), 0)
    u_pos = lax.broadcasted_iota(jnp.int32, (B, B), 1)
    same = (t_pos >= u_pos) & (seg_of(first + t_pos) == seg_of(first + u_pos))
    mask_ref[...] = jnp.where(same, 0.0, -1e30).astype(F32)
    tri = jnp.where(t_pos <= u_pos, 1.0, 0.0).astype(F32)
    cum_ref[...] = lax.dot_general(
        ld_ref[...], tri, (((1,), (0,)), ((), ())),
        preferred_element_type=F32, precision=lax.Precision.HIGHEST,
    )

    def lanes(h):
        return pl.ds(pl.multiple_of(h * LANES, LANES), LANES)

    def weight_of(h):
        cb = colb_ref[h]
        return jnp.exp(cb[B - 1 : B, :] - cb) * mout_ref[...]

    def gamma_of(h):
        return jnp.exp(colb_ref[h]) * min_ref[...]

    def passing_of(h):
        return jnp.exp(colb_ref[h, B - 1 : B, :]) * open_all

    def decay_of(h, i):
        ts, cols = slice(i * tile, (i + 1) * tile), (i + 1) * tile
        cb = colb_ref[h, ts, :]
        wide = jnp.concatenate([cb] * (cols // LANES), axis=1)
        row = cum_ref[pl.ds(h, 1), :cols]
        return jnp.exp((wide - row) + mask_ref[ts, :cols])

    def hop(src, dst, ss, rs, g, to):
        span = pl.ds(g * group, group)
        return pltpu.make_async_remote_copy(
            src_ref=src.at[span], dst_ref=dst.at[span], send_sem=ss.at[g], recv_sem=rs.at[g],
            device_id={"seq": to}, device_id_type=MESH,
        )

    def forward(g):
        return hop(fsend, frecv, fss, frs, g, me + 1)

    def backward(g):
        return hop(bsend, brecv, bss, brs, g, me - 1)

    def each_head(g, body):
        def step(i, c):
            body(g * group + i, i)
            return c
        lax.fori_loop(0, group, step, 0)

    def update_group(g, c):
        load(0, g).wait()
        load(1, g).wait()

        def one(h, i):
            colb_ref[h] = jnp.transpose(jnp.broadcast_to(cum_ref[pl.ds(h, 1), :], (LANES, B)))
            wk = (k_ref[:, lanes(h)].astype(F32) * weight_of(h)).astype(BF16)
            upd = dot(wk, v_ref[:, lanes(h)], 0, 0)
            upd_ref[h] = upd

            @pl.when(me == 0)
            def _():
                fsend[h] = upd.astype(BF16)
                frecv[h] = jnp.zeros((LANES, LANES), BF16)

            @pl.when(me == n - 1)
            def _():
                brecv[h] = jnp.zeros((LANES, LANES), BF16)

        each_head(g, one)

        @pl.when((me == 0) & (n > 1))
        def _():
            forward(g).start()
        return c

    lax.fori_loop(0, groups, update_group, 0)

    load_x.wait()

    def turn(i, c):
        span = pl.ds(pl.multiple_of(i * LANES, LANES), LANES)
        xt_ref[span, :] = jnp.transpose(x_ref[:, span])
        return c

    lax.fori_loop(0, D // LANES, turn, 0)

    def share(z, owner):
        return pl.ds(pl.multiple_of((z * 2 + owner) * rows, math.gcd(rows, LANES)), rows)

    def x_copy(z):
        return pltpu.make_async_remote_copy(
            src_ref=xt_ref.at[share(z, mate)], dst_ref=xm_ref.at[z],
            send_sem=xss.at[z], recv_sem=xrs.at[z],
            device_id={"dp": mate}, device_id_type=MESH,
        )

    def send_x(z, c):
        x_copy(z).start()
        return c

    lax.fori_loop(0, n, send_x, 0)

    def intra_group(g, c):
        load(2, g).wait()

        def one(h, i):
            for b in range(tiles):
                ts, cols = slice(b * tile, (b + 1) * tile), (b + 1) * tile
                s = dot(q_ref[ts, lanes(h)], k_ref[:cols, lanes(h)], 1, 1)
                s_bf = (s * decay_of(h, b)).astype(BF16)
                sc_ref[h, ts, :cols] = s_bf
                att_ref[h, ts, :] = dot(s_bf, v_ref[:cols, lanes(h)], 1, 0)

        each_head(g, one)

        @pl.when(me > 0)
        def _():
            forward(g).wait_recv()

        @pl.when((me > 0) & (me < n - 1))
        def _():
            def send(h, i):
                fsend[h] = (passing_of(h) * frecv[h].astype(F32) + upd_ref[h]).astype(BF16)
            each_head(g, send)
            forward(g).start()
        return c

    lax.fori_loop(0, groups, intra_group, 0)

    def attend_group(g, c):
        load(3, g).wait()

        def one(h, i):
            gamma = gamma_of(h)
            q = q_ref[:, lanes(h)]
            att = gamma * dot(q, frecv[h], 1, 0) + att_ref[h]
            inv = lax.rsqrt(jnp.mean(att * att, axis=-1, keepdims=True) + EPS)
            normed = att * inv
            wide = g_ref[:, lanes(h)].astype(F32)
            ga = (inv * (wide - normed * jnp.mean(wide * normed, axis=-1, keepdims=True))).astype(BF16)
            ga_ref[h] = ga
            gated = (q.astype(F32) * gamma).astype(BF16)
            bs = dot(gated, ga, 0, 0)
            bs_ref[h] = bs

            @pl.when(me == n - 1)
            def _():
                bsend[h] = bs.astype(BF16)

        each_head(g, one)

        @pl.when((me == n - 1) & (n > 1))
        def _():
            backward(g).start()
        return c

    lax.fori_loop(0, groups, attend_group, 0)

    def gk_copy(g):
        return pltpu.make_async_remote_copy(
            src_ref=k_ref.at[:, columns(g)], dst_ref=gm_ref.at[:, columns(g)],
            send_sem=gss.at[g], recv_sem=grs.at[g],
            device_id={"dp": mate}, device_id_type=MESH,
        )

    def relay_back(g):
        @pl.when(me < n - 1)
        def _():
            backward(g).wait_recv()

        @pl.when((me > 0) & (me < n - 1))
        def _():
            def send(h, i):
                bsend[h] = (passing_of(h) * brecv[h].astype(F32) + bs_ref[h]).astype(BF16)
            each_head(g, send)
            backward(g).start()

    def partial(z, g):
        own = dot(xt_ref[share(z, dp), :], k_ref[:, columns(g)], 1, 0)
        return own + dot(xm_ref[z], gm_ref[:, columns(g)], 1, 0)

    def term(d, z, g):
        to = me + 1 - 2 * d
        slot = jnp.where((d == 1) & (to == z), n, z)
        return pltpu.make_async_remote_copy(
            src_ref=st_ref.at[z, g], dst_ref=st_ref.at[slot, g],
            send_sem=ss.at[z, g], recv_sem=rs.at[slot, g],
            device_id={"seq": to}, device_id_type=MESH,
        )

    def arrived(slot, g):
        pltpu.make_async_remote_copy(
            src_ref=st_ref.at[slot, g], dst_ref=st_ref.at[slot, g],
            send_sem=ss.at[0, g], recv_sem=rs.at[slot, g],
            device_id={"dp": mate}, device_id_type=MESH,
        ).wait_recv()

    flip = (me >= n // 2).astype(jnp.int32)

    def route(i):
        s = i // 2
        d = (i + flip) % 2
        z = s + (1 - d) * (n - 1 - 2 * s)
        return d, z, (1 - 2 * d) * (z - me) > 0

    def scatter(g):
        def step(i, c):
            d, z, active = route(i)
            inner = (1 - d) * me + d * (n - 1 - me) > 0

            @pl.when(active)
            def _():
                total = partial(z, g)

                @pl.when(inner)
                def _():
                    arrived(z, g)
                    st_ref[z, g] = (total + st_ref[z, g].astype(F32)).astype(BF16)

                @pl.when(jnp.logical_not(inner))
                def _():
                    st_ref[z, g] = total.astype(BF16)

                term(d, z, g).start()
            return c

        lax.fori_loop(0, (n - 1) * 2, step, 0)
        out_ref[:, columns(g)] = partial(me, g)

    def grads_group(g, c):
        def one(h, i):
            gamma = gamma_of(h)
            kis, vis = [None] * tiles, [None] * tiles
            for b in range(tiles):
                ts, cols = slice(b * tile, (b + 1) * tile), (b + 1) * tile
                ga = ga_ref[h, ts, :]
                q = q_ref[ts, lanes(h)]
                gs = (dot(ga, v_ref[:cols, lanes(h)], 1, 1) * decay_of(h, b)).astype(BF16)
                gq = gamma[ts] * dot(ga, frecv[h], 1, 1) + dot(gs, k_ref[:cols, lanes(h)], 1, 0)
                ki = dot(gs, q, 0, 0)
                vi = dot(sc_ref[h, ts, :cols], ga, 0, 0)
                q_ref[ts, lanes(h)] = gq.astype(BF16)
                for j in range(b + 1):
                    js = slice(j * tile, (j + 1) * tile)
                    kis[j] = ki[js] if kis[j] is None else kis[j] + ki[js]
                    vis[j] = vi[js] if vis[j] is None else vis[j] + vi[js]
            for j in range(tiles):
                ki_ref[i, j * tile : (j + 1) * tile, :] = kis[j]
                vi_ref[i, j * tile : (j + 1) * tile, :] = vis[j]

        each_head(g, one)

        @pl.when(g == 0)
        def _():
            relay_back(0)

        def finish(h, i):
            w = weight_of(h)
            later = brecv[h]
            k = k_ref[:, lanes(h)]
            k_ref[:, lanes(h)] = (ki_ref[i] + w * dot(v_ref[:, lanes(h)], later, 1, 1)).astype(BF16)
            g_ref[:, lanes(h)] = (vi_ref[i] + w * dot(k, later, 1, 0)).astype(BF16)

        each_head(g, finish)
        gk_copy(g).start()
        store(0, g).start()
        store(1, g).start()

        @pl.when(g == 0)
        def _():
            def rest(r, c):
                relay_back(r)
                return c

            lax.fori_loop(1, groups, rest, 0)

            def have_x(z, c):
                x_copy(z).wait_recv()
                return c

            lax.fori_loop(0, n, have_x, 0)

        gk_copy(g).wait_recv()
        scatter(g)
        return c

    lax.fori_loop(0, groups, grads_group, 0)

    def settle(g):
        @pl.when(me > 0)
        def _():
            arrived(me, g)
            out_ref[:, columns(g)] += st_ref[me, g].astype(F32)

        @pl.when(me < n - 1)
        def _():
            arrived(n, g)
            out_ref[:, columns(g)] += st_ref[n, g].astype(F32)

        store(2, g).start()

    each_group(settle)

    def drain(g):
        @pl.when(me < n - 1)
        def _():
            forward(g).wait_send()

        @pl.when(me > 0)
        def _():
            backward(g).wait_send()

        gk_copy(g).wait_send()
        for a in range(3):
            store(a, g).wait()

        def step(i, c):
            d, z, active = route(i)

            @pl.when(active)
            def _():
                term(d, z, g).wait_send()
            return c

        lax.fori_loop(0, (n - 1) * 2, step, 0)

    each_group(drain)

    def sent_x(z, c):
        x_copy(z).wait_send()
        return c

    lax.fori_loop(0, n, sent_x, 0)


def layer(lengths, log_decay, x, q, k, v, g):
    heads, B = log_decay.shape
    D, F = x.shape[1], q.shape[1]
    n = lax.axis_size("seq")
    rows = D // (2 * n)
    group = math.gcd(heads, 4)
    groups = heads // group
    hbm = pl.BlockSpec(memory_space=pl.ANY)
    state = (heads, LANES, LANES)
    wide = jax.ShapeDtypeStruct((B, F), BF16)
    dma = pltpu.SemaphoreType.DMA
    return pl.pallas_call(
        functools.partial(layer_kernel, heads),
        out_shape=(wide, wide, jax.ShapeDtypeStruct((rows, F), F32)),
        in_specs=[
            pl.BlockSpec(memory_space=pltpu.SMEM), pl.BlockSpec(memory_space=pltpu.VMEM)
        ] + [hbm] * 5,
        out_specs=(hbm, hbm, hbm),
        scratch_shapes=[pltpu.VMEM((B, F), BF16)] * 4
        + [
            pltpu.VMEM((B, D), BF16),
            pltpu.VMEM((D, B), BF16),
            pltpu.VMEM((n, rows, B), BF16),
            pltpu.VMEM((B, F), BF16),
            pltpu.VMEM((n + 1, groups, rows, group * LANES), BF16),
            pltpu.VMEM((rows, F), F32),
            pltpu.VMEM((heads, B), F32),
            pltpu.VMEM((heads, B, LANES), F32),
            pltpu.VMEM((B, B), F32),
            pltpu.VMEM((B, LANES), F32),
            pltpu.VMEM((B, LANES), F32),
            pltpu.VMEM(state, F32),
            pltpu.VMEM((heads, B, LANES), F32),
            pltpu.VMEM((heads, B, B), BF16),
            pltpu.VMEM((heads, B, LANES), BF16),
            pltpu.VMEM(state, F32),
            pltpu.VMEM((group, B, LANES), F32),
            pltpu.VMEM((group, B, LANES), F32),
        ]
        + [pltpu.VMEM(state, BF16)] * 4
        + [dma((groups,))] * 4
        + [
            dma((4, groups)), dma(()), dma((3, groups)), dma((n,)), dma((n,)),
            dma((groups,)), dma((groups,)), dma((n, groups)), dma((n + 1, groups)),
        ],
        compiler_params=pltpu.CompilerParams(
            collective_id=0, has_side_effects=True, vmem_limit_bytes=62 * 1024 * 1024
        ),
        name="layer",
    )(lengths, log_decay, x, q, k, v, g)


def body(inputs, queries, keys, values, log_decay, list_lengths, grad_out):
    gq, gv, gw = layer(
        list_lengths, log_decay[0], inputs[0], queries[0], keys[0], values[0], grad_out[0]
    )
    return gq[None], gv[None], gw


def solution(mesh):
    rows = ("groups", "dp")
    wide = P(rows, "seq", "head")
    return jax.shard_map(
        body,
        mesh=mesh,
        in_specs=(
            P(rows, "seq", None), wide, wide, wide, P(rows, "head", "seq"), P(rows, None), wide,
        ),
        out_specs=(wide, wide, P(("groups", "seq", "dp"), "head")),
        check_vma=False,
    )
```

```python
import functools
import math

import jax
import jax.numpy as jnp
from jax import lax
from jax.experimental import pallas as pl
from jax.experimental.pallas import tpu as pltpu
from jax.sharding import PartitionSpec as P

EPS = 1e-06
MESH = pl.DeviceIdType.MESH
LANES = 128
F32 = jnp.float32
BF16 = jnp.bfloat16


def dot(a, b, ca, cb):
    return lax.dot_general(a, b, (((ca,), (cb,)), ((), ())), preferred_element_type=F32)


def greet(with_mate):
    barrier = pltpu.get_barrier_semaphore()
    me = lax.axis_index("seq")
    n = lax.axis_size("seq")

    @pl.when(me > 0)
    def _():
        pl.semaphore_signal(barrier, inc=1, device_id={"seq": me - 1}, device_id_type=MESH)

    @pl.when(me < n - 1)
    def _():
        pl.semaphore_signal(barrier, inc=1, device_id={"seq": me + 1}, device_id_type=MESH)

    peers = (me > 0).astype(jnp.int32) + (me < n - 1).astype(jnp.int32)
    if with_mate:
        mate = 1 - lax.axis_index("dp")
        pl.semaphore_signal(barrier, inc=1, device_id={"dp": mate}, device_id_type=MESH)
        peers = peers + 1
    pl.semaphore_wait(barrier, peers)


def layer_kernel(
    heads, ll_ref, ld_ref, x_hbm, q_hbm, k_hbm, v_hbm, g_hbm, gq_hbm, gv_hbm, gw_hbm,
    q_ref, k_ref, v_ref, g_ref, x_ref, xt_ref, xm_ref, gm_ref, st_ref, out_ref,
    cum_ref, colb_ref, mask_ref, min_ref, mout_ref, upd_ref, att_ref, sc_ref, ga_ref,
    bs_ref, ki_ref, vi_ref, fsend, frecv, bsend, brecv, fss, frs, bss, brs,
    load_sem, x_sem, store_sem, xss, xrs, gss, grs, ss, rs,
):
    n = lax.axis_size("seq")
    me = lax.axis_index("seq")
    B = q_ref.shape[0]
    group = math.gcd(heads, 4)
    groups = heads // group
    tile = math.gcd(B, 256)
    tiles = B // tile
    first = me * B
    dp = lax.axis_index("dp")
    mate = 1 - dp
    D = x_ref.shape[1]
    rows = D // (2 * n)
    width = group * LANES

    def columns(g):
        return pl.ds(pl.multiple_of(g * width, LANES), width)

    def load(a, g):
        src = (k_hbm, v_hbm, q_hbm, g_hbm)[a]
        dst = (k_ref, v_ref, q_ref, g_ref)[a]
        return pltpu.make_async_copy(
            src.at[:, columns(g)], dst.at[:, columns(g)], load_sem.at[a, g]
        )

    def store(a, g):
        src, dst = ((q_ref, gq_hbm), (g_ref, gv_hbm), (out_ref, gw_hbm))[a]
        return pltpu.make_async_copy(
            src.at[:, columns(g)], dst.at[:, columns(g)], store_sem.at[a, g]
        )

    def each_group(body):
        def step(g, c):
            body(g)
            return c
        lax.fori_loop(0, groups, step, 0)

    def load_kv(g):
        load(0, g).start()
        load(1, g).start()

    each_group(load_kv)
    load_x = pltpu.make_async_copy(x_hbm, x_ref, x_sem)
    load_x.start()
    each_group(lambda g: load(2, g).start())
    each_group(lambda g: load(3, g).start())

    greet(True)

    lengths = [ll_ref[0, i] for i in range(ll_ref.shape[1])]
    starts = [jnp.int32(0)]
    for length in lengths[:-1]:
        starts.append(starts[-1] + length)

    def seg_of(pos):
        total = (starts[0] <= pos).astype(jnp.int32)
        for s in starts[1:]:
            total = total + (s <= pos).astype(jnp.int32)
        return total

    before = seg_of(first - 1)
    end = seg_of(first + B - 1)
    seg_col = seg_of(first + lax.broadcasted_iota(jnp.int32, (B, LANES), 0))
    min_ref[...] = jnp.where(seg_col == before, 1.0, 0.0).astype(F32)
    mout_ref[...] = jnp.where(seg_col == end, 1.0, 0.0).astype(F32)
    open_all = jnp.where(jnp.full((1, LANES), end) == before, 1.0, 0.0).astype(F32)
    t_pos = lax.broadcasted_iota(jnp.int32, (B, B), 0)
    u_pos = lax.broadcasted_iota(jnp.int32, (B, B), 1)
    same = (t_pos >= u_pos) & (seg_of(first + t_pos) == seg_of(first + u_pos))
    mask_ref[...] = jnp.where(same, 0.0, -1e30).astype(F32)
    tri = jnp.where(t_pos <= u_pos, 1.0, 0.0).astype(F32)
    cum_ref[...] = lax.dot_general(
        ld_ref[...], tri, (((1,), (0,)), ((), ())),
        preferred_element_type=F32, precision=lax.Precision.HIGHEST,
    )

    def lanes(h):
        return pl.ds(pl.multiple_of(h * LANES, LANES), LANES)

    def weight_of(h):
        cb = colb_ref[h]
        return jnp.exp(cb[B - 1 : B, :] - cb) * mout_ref[...]

    def gamma_of(h):
        return jnp.exp(colb_ref[h]) * min_ref[...]

    def passing_of(h):
        return jnp.exp(colb_ref[h, B - 1 : B, :]) * open_all

    def decay_of(h, i):
        ts, cols = slice(i * tile, (i + 1) * tile), (i + 1) * tile
        cb = colb_ref[h, ts, :]
        wide = jnp.concatenate([cb] * (cols // LANES), axis=1)
        row = cum_ref[pl.ds(h, 1), :cols]
        return jnp.exp((wide - row) + mask_ref[ts, :cols])

    def hop(src, dst, ss, rs, g, to):
        span = pl.ds(g * group, group)
        return pltpu.make_async_remote_copy(
            src_ref=src.at[span], dst_ref=dst.at[span], send_sem=ss.at[g], recv_sem=rs.at[g],
            device_id={"seq": to}, device_id_type=MESH,
        )

    def forward(g):
        return hop(fsend, frecv, fss, frs, g, me + 1)

    def backward(g):
        return hop(bsend, brecv, bss, brs, g, me - 1)

    def each_head(g, body):
        def step(i, c):
            body(g * group + i, i)
            return c
        lax.fori_loop(0, group, step, 0)

    def update_group(g, c):
        load(0, g).wait()
        load(1, g).wait()

        def one(h, i):
            colb_ref[h] = jnp.transpose(jnp.broadcast_to(cum_ref[pl.ds(h, 1), :], (LANES, B)))
            wk = (k_ref[:, lanes(h)].astype(F32) * weight_of(h)).astype(BF16)
            upd = dot(wk, v_ref[:, lanes(h)], 0, 0)
            upd_ref[h] = upd

            @pl.when(me == 0)
            def _():
                fsend[h] = upd.astype(BF16)
                frecv[h] = jnp.zeros((LANES, LANES), BF16)

            @pl.when(me == n - 1)
            def _():
                brecv[h] = jnp.zeros((LANES, LANES), BF16)

        each_head(g, one)

        @pl.when((me == 0) & (n > 1))
        def _():
            forward(g).start()
        return c

    lax.fori_loop(0, groups, update_group, 0)

    load_x.wait()

    def turn(i, c):
        span = pl.ds(pl.multiple_of(i * LANES, LANES), LANES)
        xt_ref[span, :] = jnp.transpose(x_ref[:, span])
        return c

    lax.fori_loop(0, D // LANES, turn, 0)

    def share(z, owner):
        return pl.ds(pl.multiple_of((z * 2 + owner) * rows, math.gcd(rows, LANES)), rows)

    def x_copy(z):
        return pltpu.make_async_remote_copy(
            src_ref=xt_ref.at[share(z, mate)], dst_ref=xm_ref.at[z],
            send_sem=xss.at[z], recv_sem=xrs.at[z],
            device_id={"dp": mate}, device_id_type=MESH,
        )

    def send_x(z, c):
        x_copy(z).start()
        return c

    lax.fori_loop(0, n, send_x, 0)

    def attend_group(g, c):
        load(2, g).wait()

        def intra(h, i):
            for b in range(tiles):
                ts, cols = slice(b * tile, (b + 1) * tile), (b + 1) * tile
                s = dot(q_ref[ts, lanes(h)], k_ref[:cols, lanes(h)], 1, 1)
                s_bf = (s * decay_of(h, b)).astype(BF16)
                sc_ref[h, ts, :cols] = s_bf
                att_ref[i, ts, :] = dot(s_bf, v_ref[:cols, lanes(h)], 1, 0)

        each_head(g, intra)

        @pl.when(me > 0)
        def _():
            forward(g).wait_recv()

        @pl.when((me > 0) & (me < n - 1))
        def _():
            def send(h, i):
                fsend[h] = (passing_of(h) * frecv[h].astype(F32) + upd_ref[h]).astype(BF16)
            each_head(g, send)
            forward(g).start()

        load(3, g).wait()

        def one(h, i):
            gamma = gamma_of(h)
            q = q_ref[:, lanes(h)]
            att = gamma * dot(q, frecv[h], 1, 0) + att_ref[i]
            inv = lax.rsqrt(jnp.mean(att * att, axis=-1, keepdims=True) + EPS)
            normed = att * inv
            wide = g_ref[:, lanes(h)].astype(F32)
            ga = (inv * (wide - normed * jnp.mean(wide * normed, axis=-1, keepdims=True))).astype(BF16)
            ga_ref[h] = ga
            gated = (q.astype(F32) * gamma).astype(BF16)
            bs = dot(gated, ga, 0, 0)
            bs_ref[h] = bs

            @pl.when(me == n - 1)
            def _():
                bsend[h] = bs.astype(BF16)

        each_head(g, one)

        @pl.when((me == n - 1) & (n > 1))
        def _():
            backward(g).start()
        return c

    lax.fori_loop(0, groups, attend_group, 0)

    def gk_copy(g):
        return pltpu.make_async_remote_copy(
            src_ref=k_ref.at[:, columns(g)], dst_ref=gm_ref.at[:, columns(g)],
            send_sem=gss.at[g], recv_sem=grs.at[g],
            device_id={"dp": mate}, device_id_type=MESH,
        )

    def relay_back(g):
        @pl.when(me < n - 1)
        def _():
            backward(g).wait_recv()

        @pl.when((me > 0) & (me < n - 1))
        def _():
            def send(h, i):
                bsend[h] = (passing_of(h) * brecv[h].astype(F32) + bs_ref[h]).astype(BF16)
            each_head(g, send)
            backward(g).start()

    def partial(z, g):
        own = dot(xt_ref[share(z, dp), :], k_ref[:, columns(g)], 1, 0)
        return own + dot(xm_ref[z], gm_ref[:, columns(g)], 1, 0)

    def term(d, z, g):
        to = me + 1 - 2 * d
        slot = jnp.where((d == 1) & (to == z), n, z)
        return pltpu.make_async_remote_copy(
            src_ref=st_ref.at[z, g], dst_ref=st_ref.at[slot, g],
            send_sem=ss.at[z, g], recv_sem=rs.at[slot, g],
            device_id={"seq": to}, device_id_type=MESH,
        )

    def arrived(slot, g):
        pltpu.make_async_remote_copy(
            src_ref=st_ref.at[slot, g], dst_ref=st_ref.at[slot, g],
            send_sem=ss.at[0, g], recv_sem=rs.at[slot, g],
            device_id={"dp": mate}, device_id_type=MESH,
        ).wait_recv()

    flip = (me >= n // 2).astype(jnp.int32)

    def route(i):
        s = i // 2
        d = (i + flip) % 2
        z = s + (1 - d) * (n - 1 - 2 * s)
        return d, z, (1 - 2 * d) * (z - me) > 0

    def scatter(g):
        def step(i, c):
            d, z, active = route(i)
            inner = (1 - d) * me + d * (n - 1 - me) > 0

            @pl.when(active)
            def _():
                total = partial(z, g)

                @pl.when(inner)
                def _():
                    arrived(z, g)
                    st_ref[z, g] = (total + st_ref[z, g].astype(F32)).astype(BF16)

                @pl.when(jnp.logical_not(inner))
                def _():
                    st_ref[z, g] = total.astype(BF16)

                term(d, z, g).start()
            return c

        lax.fori_loop(0, (n - 1) * 2, step, 0)
        out_ref[:, columns(g)] = partial(me, g)

    def grads_group(g, c):
        def one(h, i):
            gamma = gamma_of(h)
            kis, vis = [None] * tiles, [None] * tiles
            for b in range(tiles):
                ts, cols = slice(b * tile, (b + 1) * tile), (b + 1) * tile
                ga = ga_ref[h, ts, :]
                q = q_ref[ts, lanes(h)]
                gs = (dot(ga, v_ref[:cols, lanes(h)], 1, 1) * decay_of(h, b)).astype(BF16)
                gq = gamma[ts] * dot(ga, frecv[h], 1, 1) + dot(gs, k_ref[:cols, lanes(h)], 1, 0)
                ki = dot(gs, q, 0, 0)
                vi = dot(sc_ref[h, ts, :cols], ga, 0, 0)
                q_ref[ts, lanes(h)] = gq.astype(BF16)
                for j in range(b + 1):
                    js = slice(j * tile, (j + 1) * tile)
                    kis[j] = ki[js] if kis[j] is None else kis[j] + ki[js]
                    vis[j] = vi[js] if vis[j] is None else vis[j] + vi[js]
            for j in range(tiles):
                ki_ref[i, j * tile : (j + 1) * tile, :] = kis[j]
                vi_ref[i, j * tile : (j + 1) * tile, :] = vis[j]

        each_head(g, one)

        relay_back(g)

        def finish(h, i):
            w = weight_of(h)
            later = brecv[h]
            k = k_ref[:, lanes(h)]
            k_ref[:, lanes(h)] = (ki_ref[i] + w * dot(v_ref[:, lanes(h)], later, 1, 1)).astype(BF16)
            g_ref[:, lanes(h)] = (vi_ref[i] + w * dot(k, later, 1, 0)).astype(BF16)

        each_head(g, finish)
        gk_copy(g).start()
        store(0, g).start()
        store(1, g).start()

        @pl.when(at_end)
        def _():
            ready(g)
            scatter(g)
        return c

    at_end = (me == 0) | (me == n - 1)

    def ready(g):
        @pl.when(g == 0)
        def _():
            def have_x(z, c):
                x_copy(z).wait_recv()
                return c

            lax.fori_loop(0, n, have_x, 0)

        gk_copy(g).wait_recv()

    lax.fori_loop(0, groups, grads_group, 0)

    @pl.when(jnp.logical_not(at_end))
    def _():
        def inner_group(g):
            ready(g)
            scatter(g)
        each_group(inner_group)

    def settle(g):
        @pl.when(me > 0)
        def _():
            arrived(me, g)
            out_ref[:, columns(g)] += st_ref[me, g].astype(F32)

        @pl.when(me < n - 1)
        def _():
            arrived(n, g)
            out_ref[:, columns(g)] += st_ref[n, g].astype(F32)

        store(2, g).start()

    each_group(settle)

    def drain(g):
        @pl.when(me < n - 1)
        def _():
            forward(g).wait_send()

        @pl.when(me > 0)
        def _():
            backward(g).wait_send()

        gk_copy(g).wait_send()
        for a in range(3):
            store(a, g).wait()

        def step(i, c):
            d, z, active = route(i)

            @pl.when(active)
            def _():
                term(d, z, g).wait_send()
            return c

        lax.fori_loop(0, (n - 1) * 2, step, 0)

    each_group(drain)

    def sent_x(z, c):
        x_copy(z).wait_send()
        return c

    lax.fori_loop(0, n, sent_x, 0)


def layer(lengths, log_decay, x, q, k, v, g):
    heads, B = log_decay.shape
    D, F = x.shape[1], q.shape[1]
    n = lax.axis_size("seq")
    rows = D // (2 * n)
    group = math.gcd(heads, 4)
    groups = heads // group
    hbm = pl.BlockSpec(memory_space=pl.ANY)
    state = (heads, LANES, LANES)
    wide = jax.ShapeDtypeStruct((B, F), BF16)
    dma = pltpu.SemaphoreType.DMA
    return pl.pallas_call(
        functools.partial(layer_kernel, heads),
        out_shape=(wide, wide, jax.ShapeDtypeStruct((rows, F), F32)),
        in_specs=[
            pl.BlockSpec(memory_space=pltpu.SMEM), pl.BlockSpec(memory_space=pltpu.VMEM)
        ] + [hbm] * 5,
        out_specs=(hbm, hbm, hbm),
        scratch_shapes=[pltpu.VMEM((B, F), BF16)] * 4
        + [
            pltpu.VMEM((B, D), BF16),
            pltpu.VMEM((D, B), BF16),
            pltpu.VMEM((n, rows, B), BF16),
            pltpu.VMEM((B, F), BF16),
            pltpu.VMEM((n + 1, groups, rows, group * LANES), BF16),
            pltpu.VMEM((rows, F), F32),
            pltpu.VMEM((heads, B), F32),
            pltpu.VMEM((heads, B, LANES), F32),
            pltpu.VMEM((B, B), F32),
            pltpu.VMEM((B, LANES), F32),
            pltpu.VMEM((B, LANES), F32),
            pltpu.VMEM(state, F32),
            pltpu.VMEM((group, B, LANES), F32),
            pltpu.VMEM((heads, B, B), BF16),
            pltpu.VMEM((heads, B, LANES), BF16),
            pltpu.VMEM(state, F32),
            pltpu.VMEM((group, B, LANES), F32),
            pltpu.VMEM((group, B, LANES), F32),
        ]
        + [pltpu.VMEM(state, BF16)] * 4
        + [dma((groups,))] * 4
        + [
            dma((4, groups)), dma(()), dma((3, groups)), dma((n,)), dma((n,)),
            dma((groups,)), dma((groups,)), dma((n, groups)), dma((n + 1, groups)),
        ],
        compiler_params=pltpu.CompilerParams(
            collective_id=0, has_side_effects=True, vmem_limit_bytes=62 * 1024 * 1024
        ),
        name="layer",
    )(lengths, log_decay, x, q, k, v, g)


def body(inputs, queries, keys, values, log_decay, list_lengths, grad_out):
    gq, gv, gw = layer(
        list_lengths, log_decay[0], inputs[0], queries[0], keys[0], values[0], grad_out[0]
    )
    return gq[None], gv[None], gw


def solution(mesh):
    rows = ("groups", "dp")
    wide = P(rows, "seq", "head")
    return jax.shard_map(
        body,
        mesh=mesh,
        in_specs=(
            P(rows, "seq", None), wide, wide, wide, P(rows, "head", "seq"), P(rows, None), wide,
        ),
        out_specs=(wide, wide, P(("groups", "seq", "dp"), "head")),
        check_vma=False,
    )
```

```python
import functools
import math

import jax
import jax.numpy as jnp
from jax import lax
from jax.experimental import pallas as pl
from jax.experimental.pallas import tpu as pltpu
from jax.sharding import PartitionSpec as P

EPS = 1e-06
MESH = pl.DeviceIdType.MESH
LANES = 128
F32 = jnp.float32
BF16 = jnp.bfloat16


def dot(a, b, ca, cb):
    return lax.dot_general(a, b, (((ca,), (cb,)), ((), ())), preferred_element_type=F32)


def greet(with_mate):
    barrier = pltpu.get_barrier_semaphore()
    me = lax.axis_index("seq")
    n = lax.axis_size("seq")

    @pl.when(me > 0)
    def _():
        pl.semaphore_signal(barrier, inc=1, device_id={"seq": me - 1}, device_id_type=MESH)

    @pl.when(me < n - 1)
    def _():
        pl.semaphore_signal(barrier, inc=1, device_id={"seq": me + 1}, device_id_type=MESH)

    peers = (me > 0).astype(jnp.int32) + (me < n - 1).astype(jnp.int32)
    if with_mate:
        mate = 1 - lax.axis_index("dp")
        pl.semaphore_signal(barrier, inc=1, device_id={"dp": mate}, device_id_type=MESH)
        peers = peers + 1
    pl.semaphore_wait(barrier, peers)


def layer_kernel(
    heads, ll_ref, ld_ref, x_hbm, q_hbm, k_hbm, v_hbm, g_hbm, gq_hbm, gv_hbm, gw_hbm,
    q_ref, k_ref, v_ref, g_ref, x_ref, xt_ref, xm_ref, gm_ref, st_ref, out_ref,
    cum_ref, colb_ref, mask_ref, min_ref, mout_ref, upd_ref, att_ref, sc_ref, ga_ref,
    bs_ref, ki_ref, vi_ref, fsend, frecv, bsend, brecv, fss, frs, bss, brs,
    load_sem, x_sem, store_sem, xss, xrs, gss, grs, ss, rs,
):
    n = lax.axis_size("seq")
    me = lax.axis_index("seq")
    B = q_ref.shape[0]
    group = math.gcd(heads, 2)
    groups = heads // group
    tile = math.gcd(B, 256)
    tiles = B // tile
    first = me * B
    dp = lax.axis_index("dp")
    mate = 1 - dp
    D = x_ref.shape[1]
    rows = D // (2 * n)
    width = group * LANES

    def columns(g):
        return pl.ds(pl.multiple_of(g * width, LANES), width)

    def load(a, g):
        src = (k_hbm, v_hbm, q_hbm, g_hbm)[a]
        dst = (k_ref, v_ref, q_ref, g_ref)[a]
        return pltpu.make_async_copy(
            src.at[:, columns(g)], dst.at[:, columns(g)], load_sem.at[a, g]
        )

    def store(a, g):
        src, dst = ((q_ref, gq_hbm), (g_ref, gv_hbm), (out_ref, gw_hbm))[a]
        return pltpu.make_async_copy(
            src.at[:, columns(g)], dst.at[:, columns(g)], store_sem.at[a, g]
        )

    def each_group(body):
        def step(g, c):
            body(g)
            return c
        lax.fori_loop(0, groups, step, 0)

    def load_kv(g):
        load(0, g).start()
        load(1, g).start()

    each_group(load_kv)
    load_x = pltpu.make_async_copy(x_hbm, x_ref, x_sem)
    load_x.start()
    each_group(lambda g: load(2, g).start())
    each_group(lambda g: load(3, g).start())

    greet(True)

    lengths = [ll_ref[0, i] for i in range(ll_ref.shape[1])]
    starts = [jnp.int32(0)]
    for length in lengths[:-1]:
        starts.append(starts[-1] + length)

    def seg_of(pos):
        total = (starts[0] <= pos).astype(jnp.int32)
        for s in starts[1:]:
            total = total + (s <= pos).astype(jnp.int32)
        return total

    before = seg_of(first - 1)
    end = seg_of(first + B - 1)
    seg_col = seg_of(first + lax.broadcasted_iota(jnp.int32, (B, LANES), 0))
    min_ref[...] = jnp.where(seg_col == before, 1.0, 0.0).astype(F32)
    mout_ref[...] = jnp.where(seg_col == end, 1.0, 0.0).astype(F32)
    open_all = jnp.where(jnp.full((1, LANES), end) == before, 1.0, 0.0).astype(F32)
    t_pos = lax.broadcasted_iota(jnp.int32, (B, B), 0)
    u_pos = lax.broadcasted_iota(jnp.int32, (B, B), 1)
    same = (t_pos >= u_pos) & (seg_of(first + t_pos) == seg_of(first + u_pos))
    mask_ref[...] = jnp.where(same, 0.0, -1e30).astype(F32)
    tri = jnp.where(t_pos <= u_pos, 1.0, 0.0).astype(F32)
    cum_ref[...] = lax.dot_general(
        ld_ref[...], tri, (((1,), (0,)), ((), ())),
        preferred_element_type=F32, precision=lax.Precision.HIGHEST,
    )

    def lanes(h):
        return pl.ds(pl.multiple_of(h * LANES, LANES), LANES)

    def weight_of(h):
        cb = colb_ref[h]
        return jnp.exp(cb[B - 1 : B, :] - cb) * mout_ref[...]

    def gamma_of(h):
        return jnp.exp(colb_ref[h]) * min_ref[...]

    def passing_of(h):
        return jnp.exp(colb_ref[h, B - 1 : B, :]) * open_all

    def decay_of(h, i):
        ts, cols = slice(i * tile, (i + 1) * tile), (i + 1) * tile
        cb = colb_ref[h, ts, :]
        wide = jnp.concatenate([cb] * (cols // LANES), axis=1)
        row = cum_ref[pl.ds(h, 1), :cols]
        return jnp.exp((wide - row) + mask_ref[ts, :cols])

    def hop(src, dst, ss, rs, g, to):
        span = pl.ds(g * group, group)
        return pltpu.make_async_remote_copy(
            src_ref=src.at[span], dst_ref=dst.at[span], send_sem=ss.at[g], recv_sem=rs.at[g],
            device_id={"seq": to}, device_id_type=MESH,
        )

    def forward(g):
        return hop(fsend, frecv, fss, frs, g, me + 1)

    def backward(g):
        return hop(bsend, brecv, bss, brs, g, me - 1)

    def each_head(g, body):
        def step(i, c):
            body(g * group + i, i)
            return c
        lax.fori_loop(0, group, step, 0)

    def update_group(g, c):
        load(0, g).wait()
        load(1, g).wait()

        def one(h, i):
            colb_ref[h] = jnp.transpose(jnp.broadcast_to(cum_ref[pl.ds(h, 1), :], (LANES, B)))
            wk = (k_ref[:, lanes(h)].astype(F32) * weight_of(h)).astype(BF16)
            upd = dot(wk, v_ref[:, lanes(h)], 0, 0)
            upd_ref[h] = upd

            @pl.when(me == 0)
            def _():
                fsend[h] = upd.astype(BF16)
                frecv[h] = jnp.zeros((LANES, LANES), BF16)

            @pl.when(me == n - 1)
            def _():
                brecv[h] = jnp.zeros((LANES, LANES), BF16)

        each_head(g, one)

        @pl.when((me == 0) & (n > 1))
        def _():
            forward(g).start()
        return c

    lax.fori_loop(0, groups, update_group, 0)

    def share(z, owner):
        return pl.ds(pl.multiple_of((z * 2 + owner) * rows, math.gcd(rows, LANES)), rows)

    def x_copy(z):
        return pltpu.make_async_remote_copy(
            src_ref=xt_ref.at[share(z, mate)], dst_ref=xm_ref.at[z],
            send_sem=xss.at[z], recv_sem=xrs.at[z],
            device_id={"dp": mate}, device_id_type=MESH,
        )

    def turn_inputs():
        load_x.wait()

        def turn(i, c):
            span = pl.ds(pl.multiple_of(i * LANES, LANES), LANES)
            xt_ref[span, :] = jnp.transpose(x_ref[:, span])
            return c

        lax.fori_loop(0, D // LANES, turn, 0)

        def send_x(z, c):
            x_copy(z).start()
            return c

        lax.fori_loop(0, n, send_x, 0)

    pl.when(me == n - 1)(turn_inputs)

    def attend_group(g, c):
        load(2, g).wait()

        def intra(h, i):
            for b in range(tiles):
                ts, cols = slice(b * tile, (b + 1) * tile), (b + 1) * tile
                s = dot(q_ref[ts, lanes(h)], k_ref[:cols, lanes(h)], 1, 1)
                s_bf = (s * decay_of(h, b)).astype(BF16)
                sc_ref[h, ts, :cols] = s_bf
                att_ref[i, ts, :] = dot(s_bf, v_ref[:cols, lanes(h)], 1, 0)

        each_head(g, intra)

        @pl.when(me > 0)
        def _():
            forward(g).wait_recv()

        @pl.when((me > 0) & (me < n - 1))
        def _():
            def send(h, i):
                fsend[h] = (passing_of(h) * frecv[h].astype(F32) + upd_ref[h]).astype(BF16)
            each_head(g, send)
            forward(g).start()

        load(3, g).wait()

        def one(h, i):
            gamma = gamma_of(h)
            q = q_ref[:, lanes(h)]
            att = gamma * dot(q, frecv[h], 1, 0) + att_ref[i]
            inv = lax.rsqrt(jnp.mean(att * att, axis=-1, keepdims=True) + EPS)
            normed = att * inv
            wide = g_ref[:, lanes(h)].astype(F32)
            ga = (inv * (wide - normed * jnp.mean(wide * normed, axis=-1, keepdims=True))).astype(BF16)
            ga_ref[h] = ga
            gated = (q.astype(F32) * gamma).astype(BF16)
            bs = dot(gated, ga, 0, 0)
            bs_ref[h] = bs

            @pl.when(me == n - 1)
            def _():
                bsend[h] = bs.astype(BF16)

        each_head(g, one)

        @pl.when((me == n - 1) & (n > 1))
        def _():
            backward(g).start()
        return c

    lax.fori_loop(0, groups, attend_group, 0)
    pl.when(me < n - 1)(turn_inputs)

    def gk_copy(g):
        return pltpu.make_async_remote_copy(
            src_ref=k_ref.at[:, columns(g)], dst_ref=gm_ref.at[:, columns(g)],
            send_sem=gss.at[g], recv_sem=grs.at[g],
            device_id={"dp": mate}, device_id_type=MESH,
        )

    def relay_back(g):
        @pl.when(me < n - 1)
        def _():
            backward(g).wait_recv()

        @pl.when((me > 0) & (me < n - 1))
        def _():
            def send(h, i):
                bsend[h] = (passing_of(h) * brecv[h].astype(F32) + bs_ref[h]).astype(BF16)
            each_head(g, send)
            backward(g).start()

    def partial(z, g):
        own = dot(xt_ref[share(z, dp), :], k_ref[:, columns(g)], 1, 0)
        return own + dot(xm_ref[z], gm_ref[:, columns(g)], 1, 0)

    def term(d, z, g):
        to = me + 1 - 2 * d
        slot = jnp.where((d == 1) & (to == z), n, z)
        return pltpu.make_async_remote_copy(
            src_ref=st_ref.at[z, g], dst_ref=st_ref.at[slot, g],
            send_sem=ss.at[z, g], recv_sem=rs.at[slot, g],
            device_id={"seq": to}, device_id_type=MESH,
        )

    def arrived(slot, g):
        pltpu.make_async_remote_copy(
            src_ref=st_ref.at[slot, g], dst_ref=st_ref.at[slot, g],
            send_sem=ss.at[0, g], recv_sem=rs.at[slot, g],
            device_id={"dp": mate}, device_id_type=MESH,
        ).wait_recv()

    flip = (me >= n // 2).astype(jnp.int32)

    def route(i):
        s = i // 2
        d = (i + flip) % 2
        z = s + (1 - d) * (n - 1 - 2 * s)
        return d, z, (1 - 2 * d) * (z - me) > 0

    def scatter(g):
        def step(i, c):
            d, z, active = route(i)
            inner = (1 - d) * me + d * (n - 1 - me) > 0

            @pl.when(active)
            def _():
                total = partial(z, g)

                @pl.when(inner)
                def _():
                    arrived(z, g)
                    st_ref[z, g] = (total + st_ref[z, g].astype(F32)).astype(BF16)

                @pl.when(jnp.logical_not(inner))
                def _():
                    st_ref[z, g] = total.astype(BF16)

                term(d, z, g).start()
            return c

        lax.fori_loop(0, (n - 1) * 2, step, 0)
        out_ref[:, columns(g)] = partial(me, g)

    def grads_group(g, c):
        def one(h, i):
            gamma = gamma_of(h)
            kis, vis = [None] * tiles, [None] * tiles
            for b in range(tiles):
                ts, cols = slice(b * tile, (b + 1) * tile), (b + 1) * tile
                ga = ga_ref[h, ts, :]
                q = q_ref[ts, lanes(h)]
                gs = (dot(ga, v_ref[:cols, lanes(h)], 1, 1) * decay_of(h, b)).astype(BF16)
                gq = gamma[ts] * dot(ga, frecv[h], 1, 1) + dot(gs, k_ref[:cols, lanes(h)], 1, 0)
                ki = dot(gs, q, 0, 0)
                vi = dot(sc_ref[h, ts, :cols], ga, 0, 0)
                q_ref[ts, lanes(h)] = gq.astype(BF16)
                for j in range(b + 1):
                    js = slice(j * tile, (j + 1) * tile)
                    kis[j] = ki[js] if kis[j] is None else kis[j] + ki[js]
                    vis[j] = vi[js] if vis[j] is None else vis[j] + vi[js]
            for j in range(tiles):
                ki_ref[i, j * tile : (j + 1) * tile, :] = kis[j]
                vi_ref[i, j * tile : (j + 1) * tile, :] = vis[j]

        each_head(g, one)

        relay_back(g)

        def finish(h, i):
            w = weight_of(h)
            later = brecv[h]
            k = k_ref[:, lanes(h)]
            k_ref[:, lanes(h)] = (ki_ref[i] + w * dot(v_ref[:, lanes(h)], later, 1, 1)).astype(BF16)
            g_ref[:, lanes(h)] = (vi_ref[i] + w * dot(k, later, 1, 0)).astype(BF16)

        each_head(g, finish)
        gk_copy(g).start()
        store(0, g).start()
        store(1, g).start()

        @pl.when(at_end)
        def _():
            ready(g)
            scatter(g)
        return c

    at_end = (me == 0) | (me == n - 1)

    def ready(g):
        @pl.when(g == 0)
        def _():
            def have_x(z, c):
                x_copy(z).wait_recv()
                return c

            lax.fori_loop(0, n, have_x, 0)

        gk_copy(g).wait_recv()

    lax.fori_loop(0, groups, grads_group, 0)

    @pl.when(jnp.logical_not(at_end))
    def _():
        def inner_group(g):
            ready(g)
            scatter(g)
        each_group(inner_group)

    def settle(g):
        @pl.when(me > 0)
        def _():
            arrived(me, g)
            out_ref[:, columns(g)] += st_ref[me, g].astype(F32)

        @pl.when(me < n - 1)
        def _():
            arrived(n, g)
            out_ref[:, columns(g)] += st_ref[n, g].astype(F32)

        store(2, g).start()

    each_group(settle)

    def drain(g):
        @pl.when(me < n - 1)
        def _():
            forward(g).wait_send()

        @pl.when(me > 0)
        def _():
            backward(g).wait_send()

        gk_copy(g).wait_send()
        for a in range(3):
            store(a, g).wait()

        def step(i, c):
            d, z, active = route(i)

            @pl.when(active)
            def _():
                term(d, z, g).wait_send()
            return c

        lax.fori_loop(0, (n - 1) * 2, step, 0)

    each_group(drain)

    def sent_x(z, c):
        x_copy(z).wait_send()
        return c

    lax.fori_loop(0, n, sent_x, 0)


def layer(lengths, log_decay, x, q, k, v, g):
    heads, B = log_decay.shape
    D, F = x.shape[1], q.shape[1]
    n = lax.axis_size("seq")
    rows = D // (2 * n)
    group = math.gcd(heads, 2)
    groups = heads // group
    hbm = pl.BlockSpec(memory_space=pl.ANY)
    state = (heads, LANES, LANES)
    wide = jax.ShapeDtypeStruct((B, F), BF16)
    dma = pltpu.SemaphoreType.DMA
    return pl.pallas_call(
        functools.partial(layer_kernel, heads),
        out_shape=(wide, wide, jax.ShapeDtypeStruct((rows, F), F32)),
        in_specs=[
            pl.BlockSpec(memory_space=pltpu.SMEM), pl.BlockSpec(memory_space=pltpu.VMEM)
        ] + [hbm] * 5,
        out_specs=(hbm, hbm, hbm),
        scratch_shapes=[pltpu.VMEM((B, F), BF16)] * 4
        + [
            pltpu.VMEM((B, D), BF16),
            pltpu.VMEM((D, B), BF16),
            pltpu.VMEM((n, rows, B), BF16),
            pltpu.VMEM((B, F), BF16),
            pltpu.VMEM((n + 1, groups, rows, group * LANES), BF16),
            pltpu.VMEM((rows, F), F32),
            pltpu.VMEM((heads, B), F32),
            pltpu.VMEM((heads, B, LANES), F32),
            pltpu.VMEM((B, B), F32),
            pltpu.VMEM((B, LANES), F32),
            pltpu.VMEM((B, LANES), F32),
            pltpu.VMEM(state, F32),
            pltpu.VMEM((group, B, LANES), F32),
            pltpu.VMEM((heads, B, B), BF16),
            pltpu.VMEM((heads, B, LANES), BF16),
            pltpu.VMEM(state, F32),
            pltpu.VMEM((group, B, LANES), F32),
            pltpu.VMEM((group, B, LANES), F32),
        ]
        + [pltpu.VMEM(state, BF16)] * 4
        + [dma((groups,))] * 4
        + [
            dma((4, groups)), dma(()), dma((3, groups)), dma((n,)), dma((n,)),
            dma((groups,)), dma((groups,)), dma((n, groups)), dma((n + 1, groups)),
        ],
        compiler_params=pltpu.CompilerParams(
            collective_id=0, has_side_effects=True, vmem_limit_bytes=62 * 1024 * 1024
        ),
        name="layer",
    )(lengths, log_decay, x, q, k, v, g)


def body(inputs, queries, keys, values, log_decay, list_lengths, grad_out):
    gq, gv, gw = layer(
        list_lengths, log_decay[0], inputs[0], queries[0], keys[0], values[0], grad_out[0]
    )
    return gq[None], gv[None], gw


def solution(mesh):
    rows = ("groups", "dp")
    wide = P(rows, "seq", "head")
    return jax.shard_map(
        body,
        mesh=mesh,
        in_specs=(
            P(rows, "seq", None), wide, wide, wide, P(rows, "head", "seq"), P(rows, None), wide,
        ),
        out_specs=(wide, wide, P(("groups", "seq", "dp"), "head")),
        check_vma=False,
    )
```

```python
import functools
import math

import jax
import jax.numpy as jnp
from jax import lax
from jax.experimental import pallas as pl
from jax.experimental.pallas import tpu as pltpu
from jax.sharding import PartitionSpec as P

EPS = 1e-06
MESH = pl.DeviceIdType.MESH
LANES = 128
F32 = jnp.float32
BF16 = jnp.bfloat16


def dot(a, b, ca, cb):
    return lax.dot_general(a, b, (((ca,), (cb,)), ((), ())), preferred_element_type=F32)


def greet(with_mate):
    barrier = pltpu.get_barrier_semaphore()
    me = lax.axis_index("seq")
    n = lax.axis_size("seq")

    @pl.when(me > 0)
    def _():
        pl.semaphore_signal(barrier, inc=1, device_id={"seq": me - 1}, device_id_type=MESH)

    @pl.when(me < n - 1)
    def _():
        pl.semaphore_signal(barrier, inc=1, device_id={"seq": me + 1}, device_id_type=MESH)

    peers = (me > 0).astype(jnp.int32) + (me < n - 1).astype(jnp.int32)
    if with_mate:
        mate = 1 - lax.axis_index("dp")
        pl.semaphore_signal(barrier, inc=1, device_id={"dp": mate}, device_id_type=MESH)
        peers = peers + 1
    pl.semaphore_wait(barrier, peers)


def layer_kernel(
    heads, ll_ref, ld_ref, x_hbm, q_hbm, k_hbm, v_hbm, g_hbm, gq_hbm, gv_hbm, gw_hbm,
    q_ref, k_ref, v_ref, g_ref, x_ref, xt_ref, xm_ref, gm_ref, st_ref, out_ref,
    cum_ref, colb_ref, mask_ref, min_ref, mout_ref, upd_ref, att_ref, sc_ref, ga_ref,
    bs_ref, ki_ref, vi_ref, fsend, frecv, bsend, brecv, fss, frs, bss, brs,
    load_sem, x_sem, store_sem, xss, xrs, gss, grs, ss, rs,
):
    n = lax.axis_size("seq")
    me = lax.axis_index("seq")
    B = q_ref.shape[0]
    group = math.gcd(heads, 2)
    groups = heads // group
    tile = math.gcd(B, 256)
    tiles = B // tile
    first = me * B
    dp = lax.axis_index("dp")
    mate = 1 - dp
    D = x_ref.shape[1]
    rows = D // (2 * n)
    width = group * LANES

    def columns(g):
        return pl.ds(pl.multiple_of(g * width, LANES), width)

    def load(a, g):
        src = (k_hbm, v_hbm, q_hbm, g_hbm)[a]
        dst = (k_ref, v_ref, q_ref, g_ref)[a]
        return pltpu.make_async_copy(
            src.at[:, columns(g)], dst.at[:, columns(g)], load_sem.at[a, g]
        )

    def store(a, g):
        src, dst = ((q_ref, gq_hbm), (g_ref, gv_hbm), (out_ref, gw_hbm))[a]
        return pltpu.make_async_copy(
            src.at[:, columns(g)], dst.at[:, columns(g)], store_sem.at[a, g]
        )

    def each_group(body):
        def step(g, c):
            body(g)
            return c
        lax.fori_loop(0, groups, step, 0)

    def load_kv(g):
        load(0, g).start()
        load(1, g).start()

    each_group(load_kv)
    load_x = pltpu.make_async_copy(x_hbm, x_ref, x_sem)
    load_x.start()
    each_group(lambda g: load(2, g).start())
    each_group(lambda g: load(3, g).start())

    greet(True)

    lengths = [ll_ref[0, i] for i in range(ll_ref.shape[1])]
    starts = [jnp.int32(0)]
    for length in lengths[:-1]:
        starts.append(starts[-1] + length)

    def seg_of(pos):
        total = (starts[0] <= pos).astype(jnp.int32)
        for s in starts[1:]:
            total = total + (s <= pos).astype(jnp.int32)
        return total

    before = seg_of(first - 1)
    end = seg_of(first + B - 1)
    seg_col = seg_of(first + lax.broadcasted_iota(jnp.int32, (B, LANES), 0))
    min_ref[...] = jnp.where(seg_col == before, 1.0, 0.0).astype(F32)
    mout_ref[...] = jnp.where(seg_col == end, 1.0, 0.0).astype(F32)
    open_all = jnp.where(jnp.full((1, LANES), end) == before, 1.0, 0.0).astype(F32)
    t_pos = lax.broadcasted_iota(jnp.int32, (B, B), 0)
    u_pos = lax.broadcasted_iota(jnp.int32, (B, B), 1)
    same = (t_pos >= u_pos) & (seg_of(first + t_pos) == seg_of(first + u_pos))
    mask_ref[...] = jnp.where(same, 0.0, -1e30).astype(F32)
    tri = jnp.where(t_pos <= u_pos, 1.0, 0.0).astype(F32)
    cum_ref[...] = lax.dot_general(
        ld_ref[...], tri, (((1,), (0,)), ((), ())),
        preferred_element_type=F32, precision=lax.Precision.HIGHEST,
    )

    def lanes(h):
        return pl.ds(pl.multiple_of(h * LANES, LANES), LANES)

    def weight_of(h):
        cb = colb_ref[h]
        return jnp.exp(cb[B - 1 : B, :] - cb) * mout_ref[...]

    def gamma_of(h):
        return jnp.exp(colb_ref[h]) * min_ref[...]

    def passing_of(h):
        return jnp.exp(colb_ref[h, B - 1 : B, :]) * open_all

    def decay_of(h, i):
        ts, cols = slice(i * tile, (i + 1) * tile), (i + 1) * tile
        cb = colb_ref[h, ts, :]
        wide = jnp.concatenate([cb] * (cols // LANES), axis=1)
        row = cum_ref[pl.ds(h, 1), :cols]
        return jnp.exp((wide - row) + mask_ref[ts, :cols])

    def hop(src, dst, ss, rs, g, to):
        span = pl.ds(g * group, group)
        return pltpu.make_async_remote_copy(
            src_ref=src.at[span], dst_ref=dst.at[span], send_sem=ss.at[g], recv_sem=rs.at[g],
            device_id={"seq": to}, device_id_type=MESH,
        )

    def forward(g):
        return hop(fsend, frecv, fss, frs, g, me + 1)

    def backward(g):
        return hop(bsend, brecv, bss, brs, g, me - 1)

    def each_head(g, body):
        def step(i, c):
            body(g * group + i, i)
            return c
        lax.fori_loop(0, group, step, 0)

    def update_group(g, c):
        load(0, g).wait()
        load(1, g).wait()

        def one(h, i):
            colb_ref[h] = jnp.transpose(jnp.broadcast_to(cum_ref[pl.ds(h, 1), :], (LANES, B)))
            wk = (k_ref[:, lanes(h)].astype(F32) * weight_of(h)).astype(BF16)
            upd = dot(wk, v_ref[:, lanes(h)], 0, 0)
            upd_ref[h] = upd

            @pl.when(me == 0)
            def _():
                fsend[h] = upd.astype(BF16)
                frecv[h] = jnp.zeros((LANES, LANES), BF16)

            @pl.when(me == n - 1)
            def _():
                brecv[h] = jnp.zeros((LANES, LANES), BF16)

        each_head(g, one)

        @pl.when((me == 0) & (n > 1))
        def _():
            forward(g).start()
        return c

    lax.fori_loop(0, groups, update_group, 0)

    def share(z, owner):
        return pl.ds(pl.multiple_of((z * 2 + owner) * rows, math.gcd(rows, LANES)), rows)

    def x_copy(z):
        return pltpu.make_async_remote_copy(
            src_ref=xt_ref.at[share(z, mate)], dst_ref=xm_ref.at[z],
            send_sem=xss.at[z], recv_sem=xrs.at[z],
            device_id={"dp": mate}, device_id_type=MESH,
        )

    def turn_inputs():
        load_x.wait()

        def turn(i, c):
            span = pl.ds(pl.multiple_of(i * LANES, LANES), LANES)
            xt_ref[span, :] = jnp.transpose(x_ref[:, span])
            return c

        lax.fori_loop(0, D // LANES, turn, 0)

        def send_x(z, c):
            x_copy(z).start()
            return c

        lax.fori_loop(0, n, send_x, 0)

    pl.when(me == n - 1)(turn_inputs)

    def attend_group(g, c):
        load(2, g).wait()

        def intra(h, i):
            for b in range(tiles):
                ts, cols = slice(b * tile, (b + 1) * tile), (b + 1) * tile
                s = dot(q_ref[ts, lanes(h)], k_ref[:cols, lanes(h)], 1, 1)
                s_bf = (s * decay_of(h, b)).astype(BF16)
                sc_ref[h, ts, :cols] = s_bf
                att_ref[i, ts, :] = dot(s_bf, v_ref[:cols, lanes(h)], 1, 0)

        each_head(g, intra)

        @pl.when(me > 0)
        def _():
            forward(g).wait_recv()

        @pl.when((me > 0) & (me < n - 1))
        def _():
            def send(h, i):
                fsend[h] = (passing_of(h) * frecv[h].astype(F32) + upd_ref[h]).astype(BF16)
            each_head(g, send)
            forward(g).start()

        load(3, g).wait()

        def one(h, i):
            gamma = gamma_of(h)
            q = q_ref[:, lanes(h)]
            att = gamma * dot(q, frecv[h], 1, 0) + att_ref[i]
            inv = lax.rsqrt(jnp.mean(att * att, axis=-1, keepdims=True) + EPS)
            normed = att * inv
            wide = g_ref[:, lanes(h)].astype(F32)
            ga = (inv * (wide - normed * jnp.mean(wide * normed, axis=-1, keepdims=True))).astype(BF16)
            ga_ref[h] = ga
            gated = (q.astype(F32) * gamma).astype(BF16)
            bs = dot(gated, ga, 0, 0)
            bs_ref[h] = bs

            @pl.when(me == n - 1)
            def _():
                bsend[h] = bs.astype(BF16)

        each_head(g, one)

        @pl.when((me == n - 1) & (n > 1))
        def _():
            backward(g).start()
        return c

    lax.fori_loop(0, groups, attend_group, 0)
    pl.when(me < n - 1)(turn_inputs)

    def gk_copy(g):
        return pltpu.make_async_remote_copy(
            src_ref=k_ref.at[:, columns(g)], dst_ref=gm_ref.at[:, columns(g)],
            send_sem=gss.at[g], recv_sem=grs.at[g],
            device_id={"dp": mate}, device_id_type=MESH,
        )

    def relay_back(g):
        @pl.when(me < n - 1)
        def _():
            backward(g).wait_recv()

        @pl.when((me > 0) & (me < n - 1))
        def _():
            def send(h, i):
                bsend[h] = (passing_of(h) * brecv[h].astype(F32) + bs_ref[h]).astype(BF16)
            each_head(g, send)
            backward(g).start()

    def partial(z, g):
        own = dot(xt_ref[share(z, dp), :], k_ref[:, columns(g)], 1, 0)
        return own + dot(xm_ref[z], gm_ref[:, columns(g)], 1, 0)

    def term(d, z, g):
        to = me + 1 - 2 * d
        slot = jnp.where((d == 1) & (to == z), n, z)
        return pltpu.make_async_remote_copy(
            src_ref=st_ref.at[z, g], dst_ref=st_ref.at[slot, g],
            send_sem=ss.at[z, g], recv_sem=rs.at[slot, g],
            device_id={"seq": to}, device_id_type=MESH,
        )

    def arrived(slot, g):
        pltpu.make_async_remote_copy(
            src_ref=st_ref.at[slot, g], dst_ref=st_ref.at[slot, g],
            send_sem=ss.at[0, g], recv_sem=rs.at[slot, g],
            device_id={"dp": mate}, device_id_type=MESH,
        ).wait_recv()

    flip = (me >= n // 2).astype(jnp.int32)

    def route(i):
        s = i // 2
        d = (i + flip) % 2
        z = s + (1 - d) * (n - 1 - 2 * s)
        return d, z, (1 - 2 * d) * (z - me) > 0

    def scatter(g):
        def step(i, c):
            d, z, active = route(i)
            inner = (1 - d) * me + d * (n - 1 - me) > 0

            @pl.when(active)
            def _():
                total = partial(z, g)

                @pl.when(inner)
                def _():
                    arrived(z, g)
                    st_ref[z, g] = (total + st_ref[z, g].astype(F32)).astype(BF16)

                @pl.when(jnp.logical_not(inner))
                def _():
                    st_ref[z, g] = total.astype(BF16)

                term(d, z, g).start()
            return c

        lax.fori_loop(0, (n - 1) * 2, step, 0)
        out_ref[:, columns(g)] = partial(me, g)

    def grads_group(g, c):
        def one(h, i):
            gamma = gamma_of(h)
            kis, vis = [None] * tiles, [None] * tiles
            for b in range(tiles):
                ts, cols = slice(b * tile, (b + 1) * tile), (b + 1) * tile
                ga = ga_ref[h, ts, :]
                q = q_ref[ts, lanes(h)]
                gs = (dot(ga, v_ref[:cols, lanes(h)], 1, 1) * decay_of(h, b)).astype(BF16)
                gq = gamma[ts] * dot(ga, frecv[h], 1, 1) + dot(gs, k_ref[:cols, lanes(h)], 1, 0)
                ki = dot(gs, q, 0, 0)
                vi = dot(sc_ref[h, ts, :cols], ga, 0, 0)
                q_ref[ts, lanes(h)] = gq.astype(BF16)
                for j in range(b + 1):
                    js = slice(j * tile, (j + 1) * tile)
                    kis[j] = ki[js] if kis[j] is None else kis[j] + ki[js]
                    vis[j] = vi[js] if vis[j] is None else vis[j] + vi[js]
            for j in range(tiles):
                ki_ref[i, j * tile : (j + 1) * tile, :] = kis[j]
                vi_ref[i, j * tile : (j + 1) * tile, :] = vis[j]

        each_head(g, one)

        relay_back(g)

        def finish(h, i):
            w = weight_of(h)
            later = brecv[h]
            k = k_ref[:, lanes(h)]
            k_ref[:, lanes(h)] = (ki_ref[i] + w * dot(v_ref[:, lanes(h)], later, 1, 1)).astype(BF16)
            g_ref[:, lanes(h)] = (vi_ref[i] + w * dot(k, later, 1, 0)).astype(BF16)

        each_head(g, finish)
        gk_copy(g).start()
        store(0, g).start()
        store(1, g).start()

        @pl.when(at_end)
        def _():
            ready(g)
            scatter(g)
        return c

    at_end = (me == 0) | (me == n - 1)

    def ready(g):
        @pl.when(g == 0)
        def _():
            def have_x(z, c):
                x_copy(z).wait_recv()
                return c

            lax.fori_loop(0, n, have_x, 0)

        gk_copy(g).wait_recv()

    lax.fori_loop(0, groups, grads_group, 0)

    @pl.when(jnp.logical_not(at_end))
    def _():
        def inner_group(g):
            ready(g)
            scatter(g)
        each_group(inner_group)

    def settle(g):
        @pl.when(me > 0)
        def _():
            arrived(me, g)
            out_ref[:, columns(g)] += st_ref[me, g].astype(F32)

        @pl.when(me < n - 1)
        def _():
            arrived(n, g)
            out_ref[:, columns(g)] += st_ref[n, g].astype(F32)

        store(2, g).start()

    each_group(settle)

    def drain(g):
        @pl.when(me < n - 1)
        def _():
            forward(g).wait_send()

        @pl.when(me > 0)
        def _():
            backward(g).wait_send()

        gk_copy(g).wait_send()
        for a in range(3):
            store(a, g).wait()

        def step(i, c):
            d, z, active = route(i)

            @pl.when(active)
            def _():
                term(d, z, g).wait_send()
            return c

        lax.fori_loop(0, (n - 1) * 2, step, 0)

    each_group(drain)

    def sent_x(z, c):
        x_copy(z).wait_send()
        return c

    lax.fori_loop(0, n, sent_x, 0)


def layer(lengths, log_decay, x, q, k, v, g):
    heads, B = log_decay.shape
    D, F = x.shape[1], q.shape[1]
    n = lax.axis_size("seq")
    rows = D // (2 * n)
    group = math.gcd(heads, 2)
    groups = heads // group
    hbm = pl.BlockSpec(memory_space=pl.ANY)
    state = (heads, LANES, LANES)
    wide = jax.ShapeDtypeStruct((B, F), BF16)
    dma = pltpu.SemaphoreType.DMA
    return pl.pallas_call(
        functools.partial(layer_kernel, heads),
        out_shape=(wide, wide, jax.ShapeDtypeStruct((rows, F), F32)),
        in_specs=[
            pl.BlockSpec(memory_space=pltpu.SMEM), pl.BlockSpec(memory_space=pltpu.VMEM)
        ] + [hbm] * 5,
        out_specs=(hbm, hbm, hbm),
        scratch_shapes=[pltpu.VMEM((B, F), BF16)] * 4
        + [
            pltpu.VMEM((B, D), BF16),
            pltpu.VMEM((D, B), BF16),
            pltpu.VMEM((n, rows, B), BF16),
            pltpu.VMEM((B, F), BF16),
            pltpu.VMEM((n + 1, groups, rows, group * LANES), BF16),
            pltpu.VMEM((rows, F), F32),
            pltpu.VMEM((heads, B), F32),
            pltpu.VMEM((heads, B, LANES), F32),
            pltpu.VMEM((B, B), F32),
            pltpu.VMEM((B, LANES), F32),
            pltpu.VMEM((B, LANES), F32),
            pltpu.VMEM(state, F32),
            pltpu.VMEM((group, B, LANES), F32),
            pltpu.VMEM((heads, B, B), BF16),
            pltpu.VMEM((heads, B, LANES), BF16),
            pltpu.VMEM(state, F32),
            pltpu.VMEM((group, B, LANES), F32),
            pltpu.VMEM((group, B, LANES), F32),
        ]
        + [pltpu.VMEM(state, BF16)] * 4
        + [dma((groups,))] * 4
        + [
            dma((4, groups)), dma(()), dma((3, groups)), dma((n,)), dma((n,)),
            dma((groups,)), dma((groups,)), dma((n, groups)), dma((n + 1, groups)),
        ],
        compiler_params=pltpu.CompilerParams(
            collective_id=0, has_side_effects=True, vmem_limit_bytes=62 * 1024 * 1024
        ),
        name="layer",
    )(lengths, log_decay, x, q, k, v, g)


def deliver_kernel(pieces, *refs):
    count = (len(refs) - 2) // 3
    srcs, dsts, bufs = refs[:count], refs[count : 2 * count], refs[2 * count : 3 * count]
    in_sem, out_sem = refs[3 * count :]
    spans = []
    for a in range(count):
        size = srcs[a].shape[0] // pieces
        spans += [(a, p, pl.ds(p * size, size)) for p in range(pieces)]

    def load(a, p, span):
        return pltpu.make_async_copy(srcs[a].at[span], bufs[a].at[span], in_sem.at[a, p])

    def store(a, p, span):
        return pltpu.make_async_copy(bufs[a].at[span], dsts[a].at[span], out_sem.at[a, p])

    for item in spans:
        load(*item).start()
    for item in spans:
        load(*item).wait()
        store(*item).start()
    for item in spans:
        store(*item).wait()


def deliver(*arrays):
    pieces = 4
    hbm = pl.BlockSpec(memory_space=pl.ANY)
    sems = pltpu.SemaphoreType.DMA((len(arrays), pieces))
    return pl.pallas_call(
        functools.partial(deliver_kernel, pieces),
        out_shape=tuple(jax.ShapeDtypeStruct(a.shape, a.dtype) for a in arrays),
        in_specs=[hbm] * len(arrays),
        out_specs=(hbm,) * len(arrays),
        scratch_shapes=[pltpu.VMEM(a.shape, a.dtype) for a in arrays] + [sems, sems],
        compiler_params=pltpu.CompilerParams(vmem_limit_bytes=60 * 1024 * 1024),
        name="deliver",
    )(*arrays)


def body(inputs, queries, keys, values, log_decay, list_lengths, grad_out):
    gq, gv, gw = layer(
        list_lengths, log_decay[0], inputs[0], queries[0], keys[0], values[0], grad_out[0]
    )
    gq, gv, gw = deliver(gq, gv, gw)
    return gq[None], gv[None], gw


def solution(mesh):
    rows = ("groups", "dp")
    wide = P(rows, "seq", "head")
    return jax.shard_map(
        body,
        mesh=mesh,
        in_specs=(
            P(rows, "seq", None), wide, wide, wide, P(rows, "head", "seq"), P(rows, None), wide,
        ),
        out_specs=(wide, wide, P(("groups", "seq", "dp"), "head")),
        check_vma=False,
    )
```
